256 devices in a mesh: wa: 16 (over y_hi, z), dev: 16 (over y_lo, x, core).
Axes of the slice: x: 4, y: 4 (y_hi: 2, y_lo: 2; y = y_hi * 2 + y_lo), z: 8, core: 2. Of those that a mesh axis runs over, the one named last changes fastest.
Arguments:
- output_gradient: bfloat16 [2048, 8192], P('wa'), may hold values from -6 to 6
- down_weight: bfloat16 [28672, 8192], P('dev', 'wa'), may hold values from -0.03125 to 0.03125
- gate_preactivation: bfloat16 [2048, 28672], P('wa', 'dev'), may hold values from -6 to 6
- up_preactivation: bfloat16 [2048, 28672], P('wa', 'dev'), may hold values from -6 to 6
- adapter_down_factor: bfloat16 [16, 16, 28672], P(None, None, 'dev'), may hold values from -0.0625 to 0.0625
- adapter_up_factor: bfloat16 [16, 16, 8192], P(None, None, 'dev'), may hold values from -0.0625 to 0.0625
- tile_owner_adapter: int32 [128, 1], replicated, may hold values from 0 to 15
- tile_live_count: int32 [128], replicated, may hold values from 1 to 16
Outputs:
- grad_gate: bfloat16 [2048, 28672], P('wa', 'dev')
- grad_up: bfloat16 [2048, 28672], P('wa', 'dev')
- grad_a: float32 [16, 16, 28672], P('wa', None, 'dev')
- grad_b: float32 [16, 16, 8192], P('wa', None, 'dev')
The draws below stay inside these ranges and needn't reach their ends.
Inputs may be any that keep to these rules, and one draw needn't show every extreme that they name: `tile_owner_adapter`: every one of the 16 adapters owns at least one tile.
All inputs are finite; a program needn't handle non-finite values.
Results may differ from the reference program's by a relative error of at most 0.013.
Values may be sent and summed in bfloat16 or wider, within the bound.
A program may use at most 128 MiB of HBM per device.

```python
import jax
import jax.numpy as jnp
from jax import lax

MODEL_WIDTH = 8192
HIDDEN_UNITS = 28672
ADAPTER_RANK = 16
ADAPTER_COUNT = 16
TILE = 16
TOKENS = 2048
TILES = 128
N_WA = 16


def set_ends(drawn, rng, least, high):
    spot = [jax.random.randint(jax.random.fold_in(rng, axis), (), 0, length) for axis, length in enumerate(drawn.shape)]
    widest = drawn.shape.index(max(drawn.shape))
    next_to = spot[:widest] + [(spot[widest] + 1) % drawn.shape[widest]] + spot[widest + 1:]
    return drawn.at[tuple(spot)].set(least).at[tuple(next_to)].set(high)


def spiked(values, rng, source, target, shards_of, factor):
    owner, partner = [(jnp.arange(values.shape[axis_at]) // (values.shape[axis_at] // shards_of)).reshape([-1 if axis == axis_at else 1 for axis in range(values.ndim)]) for axis_at in (source, target)]
    chosen = jax.random.permutation(rng, shards_of)[partner]
    strong = (owner == chosen) | (owner == (partner + shards_of // 2) % shards_of)
    return jnp.where(strong, factor * values, values)


def block_levels(rng, extent, shards, low, high):
    level = 1.0
    for axis_at, shards_of in shards:
        heights = jax.random.uniform(jax.random.fold_in(jax.random.fold_in(rng, 6), axis_at), (shards_of,), jnp.float32, low / len(shards), high / len(shards))
        level = level * jnp.repeat(jnp.exp(heights), extent[axis_at] // shards_of).reshape((-1,) + (1,) * (len(extent) - 1 - axis_at))
    return level


def choose_distinct(own_key, rows, number_of, top, lift):
    sequence = jax.random.permutation(jax.random.fold_in(own_key, 1), number_of)
    favour = sequence
    for power in range(3):
        favour = favour * favour // number_of
    favour = favour * lift // number_of
    lots = jax.random.randint(jax.random.fold_in(own_key, 2), (rows, number_of), 0, 4096) + favour
    holders = jax.random.permutation(jax.random.fold_in(own_key, 3), rows)[jnp.arange(number_of) % rows]
    lots = jnp.where(jnp.arange(rows)[:, None] == holders[None, :], 1 << 14, lots)
    score = lots * number_of + jnp.arange(number_of)
    return lax.top_k(score.astype(jnp.int32), top)[1].astype(jnp.int32)


def bell_draw(own_key, extent, scale, reach, pieces=(), kind=jnp.bfloat16):
    entries = jax.random.normal(own_key, extent, jnp.float32) * scale
    if len(pieces) > 0:
        entries = block_levels(own_key, extent, pieces, -0.22, 0.18) * entries
    return jnp.clip(entries, min=-reach, max=reach).astype(kind)


def gaussian_with(own_key, dims, spread, reach, pieces, heavy, kind=jnp.bfloat16):
    values = spread * jax.random.normal(own_key, dims, jnp.float32)
    if pieces:
        values = values * block_levels(own_key, dims, pieces, -0.22, 0.18)
    return jnp.clip(spiked(values, jax.random.fold_in(own_key, 3), *heavy), -reach, reach).astype(kind)


def setup_inputs(seed: int = 0) -> dict:
    seeds = jax.random.split(jax.random.key(seed), 9)
    output_gradient = gaussian_with(seeds[0], (TOKENS, MODEL_WIDTH), 1.0, 6.0, ((0, 16),), (1, 0, 16, 2.0))
    down_weight = bell_draw(seeds[1], (HIDDEN_UNITS, MODEL_WIDTH), HIDDEN_UNITS ** -0.5, 0.03125, ((0, 16), (1, 16)))
    gate_preactivation = bell_draw(seeds[2], (TOKENS, HIDDEN_UNITS), 1.0, 6.0, ((0, 16), (1, 16)))
    up_preactivation = bell_draw(seeds[3], (TOKENS, HIDDEN_UNITS), 1.0, 6.0, ((0, 16), (1, 16)))
    adapter_down_factor = bell_draw(seeds[4], (ADAPTER_COUNT, ADAPTER_RANK, HIDDEN_UNITS), (HIDDEN_UNITS // 4) ** -0.5, 0.0625, ((2, 16),))
    adapter_up_factor = bell_draw(seeds[5], (ADAPTER_COUNT, ADAPTER_RANK, MODEL_WIDTH), MODEL_WIDTH ** -0.5, 0.0625, ((2, 16),))
    tile_owner_adapter = choose_distinct(seeds[6], TILES, ADAPTER_COUNT, 1, 1024)
    tile_live_count = set_ends(jax.random.randint(seeds[7], (TILES,), 1, TILE + 1), jax.random.fold_in(seeds[7], 1), 1, TILE).astype(jnp.int32)
    return dict(output_gradient=output_gradient, down_weight=down_weight, gate_preactivation=gate_preactivation, up_preactivation=up_preactivation, adapter_down_factor=adapter_down_factor, adapter_up_factor=adapter_up_factor, tile_owner_adapter=tile_owner_adapter, tile_live_count=tile_live_count)


def reference(output_gradient, down_weight, gate_preactivation, up_preactivation, adapter_down_factor, adapter_up_factor, tile_owner_adapter, tile_live_count):
    row_adapter = jnp.repeat(tile_owner_adapter[:, 0], TILE)
    position = (jnp.arange(TOKENS) % TILE).astype(jnp.int32)
    live_rows = position < jnp.repeat(tile_live_count, TILE)
    masked_rows = jnp.where(live_rows[:, None], output_gradient, jnp.zeros((), output_gradient.dtype))
    gate_wide = gate_preactivation.astype(jnp.float32)
    up_wide = up_preactivation.astype(jnp.float32)
    hidden_state = (jax.nn.silu(gate_wide) * up_wide).astype(jnp.bfloat16)
    group_width = MODEL_WIDTH // N_WA

    def add_group(group_number, running):
        offset = (group_number * group_width).astype(jnp.int32)
        columns = lax.dynamic_slice_in_dim(masked_rows, offset, group_width, 1)
        weights = lax.dynamic_slice_in_dim(down_weight, offset, group_width, 1)
        partial_value = lax.dot_general(columns, weights, (((1,), (1,)), ((), ())), preferred_element_type=jnp.float32)
        rounded = lax.optimization_barrier(partial_value.astype(jnp.bfloat16))
        return running + rounded.astype(jnp.float32)

    base_grad = lax.fori_loop(0, N_WA, add_group, jnp.zeros((TOKENS, HIDDEN_UNITS), jnp.float32))
    selector = row_adapter[:, None] == jnp.arange(ADAPTER_COUNT, dtype=jnp.int32)[None, :]
    flattened_down = adapter_down_factor.reshape(ADAPTER_COUNT * ADAPTER_RANK, HIDDEN_UNITS)
    flattened_up = adapter_up_factor.reshape(ADAPTER_COUNT * ADAPTER_RANK, MODEL_WIDTH)

    def choose_rows(complete_value):
        reshaped_value = complete_value.reshape(TOKENS, ADAPTER_COUNT, ADAPTER_RANK)
        return jnp.sum(jnp.where(selector[:, :, None], reshaped_value, jnp.zeros((), complete_value.dtype)), axis=1)

    def spread_value(values):
        wide_value = jnp.where(selector[:, :, None], values[:, None, :], jnp.zeros((), values.dtype))
        return wide_value.reshape(TOKENS, ADAPTER_COUNT * ADAPTER_RANK)

    adapter_input = choose_rows(lax.dot_general(hidden_state, flattened_down, (((1,), (1,)), ((), ())), preferred_element_type=jnp.float32)).astype(jnp.bfloat16)
    adapter_output = choose_rows(lax.dot_general(masked_rows, flattened_up, (((1,), (1,)), ((), ())), preferred_element_type=jnp.float32)).astype(jnp.bfloat16)
    spread_output = spread_value(adapter_output)
    spread_input = spread_value(adapter_input)
    hidden_grad = base_grad + 2.0 * jnp.dot(spread_output, flattened_down, preferred_element_type=jnp.float32)
    sigmoid_gate = jax.nn.sigmoid(gate_wide)
    grad_up = (hidden_grad * gate_wide * sigmoid_gate).astype(jnp.bfloat16)
    grad_gate = (hidden_grad * up_wide * sigmoid_gate * (1.0 + gate_wide * (1.0 - sigmoid_gate))).astype(jnp.bfloat16)
    grad_a = 2.0 * lax.dot_general(spread_output, hidden_state, (((0,), (0,)), ((), ())), preferred_element_type=jnp.float32)
    grad_b = 2.0 * lax.dot_general(spread_input, masked_rows, (((0,), (0,)), ((), ())), preferred_element_type=jnp.float32)
    return grad_gate, grad_up, grad_a.reshape(ADAPTER_COUNT, ADAPTER_RANK, HIDDEN_UNITS), grad_b.reshape(ADAPTER_COUNT, ADAPTER_RANK, MODEL_WIDTH)
```

```python
import jax
import jax.numpy as jnp
from jax import lax
from jax.experimental import pallas as pl
from jax.experimental.pallas import tpu as pltpu
from jax.sharding import PartitionSpec as P

TILE = 16
NZ, NY, NX, NC = 8, 4, 4, 2
NDEV = 16
ROWS = 128
KG = 512
HID = 1792
CH = 128
NCH = HID // CH
NPAIR = NCH // 2
RANK = 16
ADAPTERS = 16
AR = RANK * ADAPTERS
MESH = pl.DeviceIdType.MESH
NT = (((1,), (1,)), ((), ()))
F32 = jnp.float32
BF16 = jnp.bfloat16
OFFSETS = (0, 1, 7, 2, 6, 3, 5, 4)


def sigmoid(v):
    return 1.0 / (1.0 + jnp.exp(-v))


def kernel(
    g_ref, w_ref, gate_ref, up_ref, a_ref, b_ref, owner_ref, live_ref,
    ogate_ref, oup_ref, oga_ref, ogb_ref,
    gs, gf, wu, wd, w2, hid, part, rbuf, sbuf, pg, rg, sg, tg, tb, gr, gsl, lo, lb, sel,
    w1_s, w1_r, wr_s, wr_r, z_s, z_r, x_s, x_r, xr_s, xr_r, c_s, c_r, l_s, l_r,
    b_s, b_r, a_s, a_r, y_s, y_r,
):
    wa = lax.axis_index("wa")
    dev = lax.axis_index("dev")
    yh, z = lax.div(wa, NZ), lax.rem(wa, NZ)
    yl, low = lax.div(dev, 8), lax.rem(dev, 8)
    x, c = lax.div(low, 2), lax.rem(low, 2)
    sh = c * 4 + x
    y = yh * 2 + yl

    def y_device(step):
        other = lax.rem(y + step, NY)
        return (lax.div(other, 2) * NZ + z, lax.rem(other, 2) * 8 + low)

    up_dev, down_dev, far_dev = y_device(1), y_device(3), y_device(2)

    def z_device(off):
        return (yh * NZ + lax.rem(z + off, NZ), dev)

    def x_index(step):
        return lax.rem(x + step, NX)

    def x_device(step):
        return (wa, yl * 8 + x_index(step) * 2 + c)

    core_dev = (wa, yl * 8 + x * 2 + (1 - c))

    def dev_device(off):
        return (wa, lax.rem(dev + off, NDEV))

    def copy(src, dst, ssem, rsem, target):
        return pltpu.make_async_remote_copy(
            src_ref=src, dst_ref=dst, send_sem=ssem, recv_sem=rsem,
            device_id=target, device_id_type=MESH,
        )

    barrier = pltpu.get_barrier_semaphore()
    peers = [z_device(o) for o in range(1, NZ)] + [dev_device(o) for o in range(1, NDEV)]
    peers += [up_dev, down_dev, far_dev]
    for peer in peers:
        pl.semaphore_signal(barrier, inc=1, device_id=peer, device_id_type=MESH)

    live = live_ref[...].astype(F32)
    tile_lane = lax.broadcasted_iota(jnp.int32, (1, 128), 1)
    share_live = jnp.sum(
        jnp.where(tile_lane == wa * 8 + sh, live, 0.0), axis=1, keepdims=True
    )
    row16 = lax.broadcasted_iota(jnp.int32, (TILE, KG), 0).astype(F32)
    keep16 = row16 < share_live
    for q in range(NZ):
        for h in range(2):
            group = (yh if h == 0 else 1 - yh) * NZ + q
            cols = pl.ds(pl.multiple_of(group * KG, KG), KG)
            rows = pl.ds(pl.multiple_of(sh * TILE, TILE), TILE)
            piece = jnp.where(keep16, g_ref[rows, cols], jnp.zeros((), BF16))
            gs[q, :, h * KG : (h + 1) * KG] = piece
    gf[pl.ds(z, 1), pl.ds(sh, 1)] = gs[pl.ds(z, 1)].reshape(1, 1, TILE, 2 * KG)

    def w_first(j):
        copy(w_ref.at[pl.ds(pl.multiple_of(2 * j * CH, CH), CH)], wu.at[j],
             w1_s.at[0, j], w1_r.at[0, j], up_dev).start()
        copy(w_ref.at[pl.ds(pl.multiple_of((2 * j + 1) * CH, CH), CH)], wd.at[j],
             w1_s.at[1, j], w1_r.at[1, j], down_dev).start()

    def w_relay(j):
        r0 = copy(wu.at[j], w2.at[2 * j], wr_s.at[0, j], wr_r.at[0, j], up_dev)
        r1 = copy(wd.at[j], w2.at[2 * j + 1], wr_s.at[1, j], wr_r.at[1, j], down_dev)
        return r0, r1

    def w_step(j):
        for d, buf, target in ((0, wu, up_dev), (1, wd, down_dev)):
            copy(buf.at[j], buf.at[j], w1_s.at[d, j], w1_r.at[d, j], target).wait_recv()
        r0, r1 = w_relay(j)
        r0.start()
        r1.start()

    def z_send(off):
        zt = lax.rem(z + off, NZ)
        return copy(gs.at[zt], gf.at[z, sh], z_s.at[off], z_r.at[off], z_device(off))

    def source(q):
        return lax.rem(z + OFFSETS[q], NZ)

    def share_of(step):
        return c * 4 + x_index(step)

    def x_send(q, d):
        band = gf.at[source(q), sh]
        return copy(band, band, x_s.at[d, q], x_r.at[d, q], x_device(1 if d == 0 else 3))

    def x_recv(q, d):
        band = gf.at[source(q), share_of(3 if d == 0 else 1)]
        return copy(band, band, x_s.at[d, q], x_r.at[d, q], x_device(1 if d == 0 else 3))

    def x_relay(q):
        if q % 2 == 0:
            band, target = gf.at[source(q), share_of(3)], x_device(1)
        else:
            band, target = gf.at[source(q), share_of(1)], x_device(3)
        return copy(band, band, xr_s.at[q], xr_r.at[q], target)

    def x_relay_recv(q):
        band = gf.at[source(q), share_of(2)]
        return copy(band, band, xr_s.at[q], xr_r.at[q], x_device(1))

    def core_send(q):
        block = gf.at[source(q), pl.ds(c * 4, 4)]
        return copy(block, block, c_s.at[q], c_r.at[q], core_dev)

    def core_recv(q):
        block = gf.at[source(q), pl.ds((1 - c) * 4, 4)]
        return copy(block, block, c_s.at[q], c_r.at[q], core_dev)

    def stage_a(q):
        if q > 0:
            off = NZ - OFFSETS[q]
            band = gf.at[source(q), sh]
            copy(band, band, z_s.at[off], z_r.at[off], z_device(off)).wait_recv()
        x_send(q, 0).start()
        x_send(q, 1).start()

    def stage_b(q):
        x_recv(q, 0).wait_recv()
        x_recv(q, 1).wait_recv()
        x_relay(q).start()

    def stage_c(q):
        x_relay_recv(q).wait_recv()
        core_send(q).start()

    def g_tick(t):
        if t < NZ:
            stage_a(t)
        if 0 <= t - 1 < NZ:
            stage_b(t - 1)
        if 0 <= t - 2 < NZ:
            stage_c(t - 2)
        if 0 <= t - 3 < NZ:
            core_recv(t - 3).wait_recv()

    pl.semaphore_wait(barrier, len(peers))
    for off in (4, 3, 5, 2, 6, 1, 7):
        z_send(off).start()
    for j in range(3):
        w_first(j)
    g_tick(0)

    def hidden_step(k, acc):
        cols = pl.ds(pl.multiple_of(k * 256, 256), 256)
        gate = gate_ref[:, cols].astype(F32)
        value = (gate * sigmoid(gate) * up_ref[:, cols].astype(F32)).astype(BF16)
        hid[:, cols] = value
        return acc + lax.dot_general(a_ref[:, cols], value, NT, preferred_element_type=F32)

    in_full = lax.fori_loop(0, HID // 256, hidden_step, jnp.zeros((AR, ROWS), F32))
    lane_tile = lax.broadcasted_iota(jnp.int32, (ROWS, 128), 1)
    sub_row = lax.broadcasted_iota(jnp.int32, (ROWS, 128), 0)
    pick = lane_tile == wa * 8 + lax.shift_right_logical(sub_row, 4)
    row_live = jnp.sum(jnp.where(pick, live, 0.0), axis=1, keepdims=True)
    position = lax.rem(lax.broadcasted_iota(jnp.int32, (ROWS, KG), 0), TILE).astype(F32)
    own_cols = pl.ds(pl.multiple_of(dev * KG, KG), KG)
    sliced = jnp.where(position < row_live, g_ref[:, own_cols], jnp.zeros((), BF16))
    gsl[...] = sliced
    out_full = lax.dot_general(b_ref[...], sliced, NT, preferred_element_type=F32)
    pick_t = sub_row == wa * 8 + lax.shift_right_logical(lane_tile, 4)
    owner_lane = jnp.sum(
        jnp.where(pick_t, owner_ref[...].astype(F32), 0.0), axis=0, keepdims=True
    )
    adapter_row = lax.shift_right_logical(
        lax.broadcasted_iota(jnp.int32, (AR, ROWS), 0), 4
    ).astype(F32)
    selected = jnp.where(adapter_row == owner_lane, 1.0, 0.0)
    sel[...] = selected

    def choose(full):
        kept = jnp.where(selected > 0.5, full, 0.0)
        return jnp.sum(kept.reshape(ADAPTERS, RANK, ROWS), axis=0)

    lb[0, 0:RANK] = choose(in_full)
    lb[0, RANK : 2 * RANK] = choose(out_full)

    def l_copy(off):
        return copy(lb.at[0], lb.at[off], l_s.at[off], l_r.at[off], dev_device(off))

    for off in range(1, NDEV):
        l_copy(off).start()

    for t in range(1, 5):
        g_tick(t)
    w_step(0)
    w_first(3)
    for t in range(5, 8):
        g_tick(t)

    for off in range(1, NDEV):
        l_copy(off).wait_recv()
    total = jnp.zeros((2 * RANK, ROWS), F32)
    for src in range(NDEV):
        total = total + lb[lax.rem(dev + NDEV - src, NDEV)]
    summed = total.astype(BF16).astype(F32)
    keep = sel[...] > 0.5

    def spread(values):
        wide = jnp.broadcast_to(values[None], (ADAPTERS, RANK, ROWS)).reshape(AR, ROWS)
        return jnp.where(keep, wide, 0.0)

    spread_in = spread(summed[0:RANK]).astype(BF16)
    spread_out_wide = spread(summed[RANK : 2 * RANK])
    spread_out = spread_out_wide.astype(BF16)
    spread_out_t = spread_out_wide.T.astype(BF16)

    def adapter_step(k, carry):
        cols = pl.ds(pl.multiple_of(k * 256, 256), 256)
        grad = 2.0 * jnp.dot(spread_out, hid[:, cols], preferred_element_type=F32)
        pg[:, :, cols] = grad.reshape(ADAPTERS, RANK, 256)
        lo[:, cols] = 2.0 * jnp.dot(spread_out_t, a_ref[:, cols], preferred_element_type=F32)
        return carry

    lax.fori_loop(0, HID // 256, adapter_step, 0)
    grad_b = 2.0 * jnp.dot(spread_in, gsl[...], preferred_element_type=F32)
    pg[:, :, HID : HID + KG] = grad_b.reshape(ADAPTERS, RANK, KG)

    w_step(1)
    w_first(4)
    for t in range(8, NZ + 3):
        g_tick(t)

    def z_next(d):
        return (yh * NZ + lax.rem(z + 1 + 6 * d, NZ), dev)

    def target_z(d, s):
        return lax.rem(z + NZ + (4 - s) * (1 - 2 * d), NZ)

    def b_copy(src, d, ch, s):
        return copy(src, rbuf.at[d, ch, s], b_s.at[d, ch, s], b_r.at[d, ch, s], z_next(d))

    def a_copy(src, d, k, s):
        return copy(src, rg.at[d, k, s], a_s.at[d, k, s], a_r.at[d, k, s], z_next(d))

    def base_first(ch, d, s):
        sbuf[ch, s] = part[ch, target_z(d, s)].astype(BF16)
        b_copy(sbuf.at[ch, s], d, ch, s).start()

    def base_forward(ch, d, s):
        slot = rbuf.at[d, ch, s - 1]
        b_copy(slot, d, ch, s - 1).wait_recv()
        slot[...] = (slot[...].astype(F32) + part[ch, target_z(d, s)]).astype(BF16)
        b_copy(slot, d, ch, s).start()

    def base_last(ch):
        for d in range(2):
            b_copy(rbuf.at[d, ch, 3], d, ch, 3).wait_recv()
        cols = pl.ds(pl.multiple_of(ch * CH, CH), CH)
        base = part[ch, z] + rbuf[0, ch, 3].astype(F32) + rbuf[1, ch, 3].astype(F32)
        grad = base + lo[:, cols]
        gate = gate_ref[:, cols].astype(F32)
        up_value = up_ref[:, cols].astype(F32)
        s = sigmoid(gate)
        oup_ref[:, cols] = (grad * gate * s).astype(BF16)
        ogate_ref[:, cols] = (grad * up_value * s * (1.0 + gate * (1.0 - s))).astype(BF16)

    def adapter_first(k, d, s):
        sg[k, s] = pg[k * NZ + target_z(d, s)].astype(BF16)
        a_copy(sg.at[k, s], d, k, s).start()

    def adapter_forward(k, d, s):
        slot = rg.at[d, k, s - 1]
        a_copy(slot, d, k, s - 1).wait_recv()
        slot[...] = (slot[...].astype(F32) + pg[k * NZ + target_z(d, s)]).astype(BF16)
        a_copy(slot, d, k, s).start()

    def adapter_last(k):
        for d in range(2):
            a_copy(rg.at[d, k, 3], d, k, 3).wait_recv()
        done = pg[k * NZ + z] + rg[0, k, 3].astype(F32) + rg[1, k, 3].astype(F32)
        tg[k] = done
        tb[k] = done.astype(BF16)

    def adapter_out():
        return copy(tb.at[1 - yh], gr, y_s, y_r, far_dev)

    def product(j):
        for d, target in ((0, up_dev), (1, down_dev)):
            got = w2.at[2 * j + d]
            copy(got, got, wr_s.at[d, j], wr_r.at[d, j], target).wait_recv()
        rows = pl.ds(pl.multiple_of(j * 2 * CH, CH), 2 * CH)
        mine = w_ref[rows, :]
        other = w2[pl.ds(2 * j, 2)].reshape(2 * CH, KG)

        def block(k, carry):
            left = gf[pl.ds(2 * k, 2)].reshape(2 * ROWS, 2 * KG)
            value = lax.dot_general(left[:, :KG], mine, NT, preferred_element_type=F32)
            value = value + lax.dot_general(left[:, KG:], other, NT, preferred_element_type=F32)
            value = value.reshape(2, ROWS, 2 * CH)
            part[2 * j, pl.ds(2 * k, 2)] = value[:, :, :CH]
            part[2 * j + 1, pl.ds(2 * k, 2)] = value[:, :, CH:]
            return carry

        lax.fori_loop(0, NZ // 2, block, 0)

    def tick(t, carry):
        for k in range(2):
            for s in (1, 2, 3):
                @pl.when(t == k + s)
                def _(k=k, s=s):
                    d4 = k % 2
                    adapter_forward(k, d4, s)
                    if s == 1:
                        adapter_first(k, 1 - d4, s)
                    else:
                        adapter_forward(k, 1 - d4, s)

            @pl.when(t == k)
            def _(k=k):
                adapter_first(k, k % 2, 0)

        for s in (3, 2, 1):
            ch = t - s

            @pl.when((ch >= 0) & (ch < NCH))
            def _(ch=ch, s=s):
                d4 = lax.rem(ch, 2)
                base_forward(ch, d4, s)
                if s == 1:
                    base_first(ch, 1 - d4, s)
                else:
                    base_forward(ch, 1 - d4, s)

        @pl.when((t < NCH) & (lax.rem(t, 2) == 0))
        def _():
            product(lax.div(t, 2))

        @pl.when(t < NCH)
        def _():
            base_first(t, lax.rem(t, 2), 0)

        ch = t - 4

        @pl.when(ch >= 0)
        def _():
            base_last(ch)

        @pl.when((lax.rem(t, 2) == 1) & (t < 10))
        def _():
            j = lax.div(t - 1, 2) + 2
            w_step(j)

            @pl.when(j + 3 < NPAIR)
            def _():
                w_first(j + 3)

        for k in range(2):
            @pl.when(t == k + 4)
            def _(k=k):
                adapter_last(k)

        @pl.when(t == 6)
        def _():
            adapter_out().start()

        return carry

    lax.fori_loop(0, NCH + 4, tick, 0)

    adapter_out().wait_recv()
    final = tg[yh] + gr[...].astype(F32)
    oga_ref[...] = final[:, :HID]
    ogb_ref[...] = final[:, HID:]

    adapter_out().wait_send()
    for off in range(1, NZ):
        z_send(off).wait_send()
    for off in range(1, NDEV):
        l_copy(off).wait_send()
    for q in range(NZ):
        x_send(q, 0).wait_send()
        x_send(q, 1).wait_send()
        x_relay(q).wait_send()
        core_send(q).wait_send()
    for k in range(2):
        for d in range(2):
            for s in range(4):
                if s > 0 or d == k % 2:
                    a_copy(rg.at[d, k, s], d, k, s).wait_send()

    def drain_w(j, carry):
        for d, buf, target in ((0, wu, up_dev), (1, wd, down_dev)):
            copy(buf.at[j], buf.at[j], w1_s.at[d, j], w1_r.at[d, j], target).wait_send()
        r0, r1 = w_relay(j)
        r0.wait_send()
        r1.wait_send()
        return carry

    lax.fori_loop(0, NPAIR, drain_w, 0)

    def drain_b(ch, carry):
        d4 = lax.rem(ch, 2)
        b_copy(rbuf.at[d4, ch, 0], d4, ch, 0).wait_send()
        for d in range(2):
            for s in range(1, 4):
                b_copy(rbuf.at[d, ch, s], d, ch, s).wait_send()
        return carry

    lax.fori_loop(0, NCH, drain_b, 0)


def on_device(grad, weight, gate, up, down_factor, up_factor, owner, live):
    dma = pltpu.SemaphoreType.DMA
    vmem = pltpu.VMEM
    whole = pl.BlockSpec(memory_space=pltpu.VMEM)
    outs = pl.pallas_call(
        kernel,
        out_shape=(
            jax.ShapeDtypeStruct((ROWS, HID), BF16),
            jax.ShapeDtypeStruct((ROWS, HID), BF16),
            jax.ShapeDtypeStruct((RANK, HID), F32),
            jax.ShapeDtypeStruct((RANK, KG), F32),
        ),
        in_specs=[whole] * 8,
        out_specs=(whole,) * 4,
        scratch_shapes=[
            vmem((NZ, TILE, 2 * KG), BF16),
            vmem((NZ, 8, TILE, 2 * KG), BF16),
            vmem((NPAIR, CH, KG), BF16),
            vmem((NPAIR, CH, KG), BF16),
            vmem((NCH, CH, KG), BF16),
            vmem((ROWS, HID), BF16),
            vmem((NCH, NZ, ROWS, CH), F32),
            vmem((2, NCH, 4, ROWS, CH), BF16),
            vmem((NCH, 2, ROWS, CH), BF16),
            vmem((ADAPTERS, RANK, HID + KG), F32),
            vmem((2, 2, 4, RANK, HID + KG), BF16),
            vmem((2, 2, RANK, HID + KG), BF16),
            vmem((2, RANK, HID + KG), F32),
            vmem((2, RANK, HID + KG), BF16),
            vmem((RANK, HID + KG), BF16),
            vmem((ROWS, KG), BF16),
            vmem((ROWS, HID), F32),
            vmem((NDEV, 2 * RANK, ROWS), F32),
            vmem((AR, ROWS), F32),
            dma((2, NPAIR)), dma((2, NPAIR)),
            dma((2, NPAIR)), dma((2, NPAIR)),
            dma((NZ,)), dma((NZ,)),
            dma((2, NZ)), dma((2, NZ)),
            dma((NZ,)), dma((NZ,)),
            dma((NZ,)), dma((NZ,)),
            dma((NDEV,)), dma((NDEV,)),
            dma((2, NCH, 4)), dma((2, NCH, 4)),
            dma((2, 2, 4)), dma((2, 2, 4)),
            dma, dma,
        ],
        compiler_params=pltpu.CompilerParams(
            collective_id=0, has_side_effects=True, vmem_limit_bytes=60 * 1024 * 1024
        ),
    )(
        grad, weight, gate, up,
        down_factor.reshape(AR, HID), up_factor.reshape(AR, KG),
        owner, live.reshape(1, live.shape[0]),
    )
    out_gate, out_up, grad_a, grad_b = outs
    return out_gate, out_up, grad_a[None], grad_b[None]


def solution(mesh):
    placed = (
        P("wa", None),
        P("dev", "wa"),
        P("wa", "dev"),
        P("wa", "dev"),
        P(None, None, "dev"),
        P(None, None, "dev"),
        P(),
        P(),
    )
    return jax.shard_map(
        on_device,
        mesh=mesh,
        in_specs=placed,
        out_specs=(P("wa", "dev"), P("wa", "dev"), P("wa", None, "dev"), P("wa", None, "dev")),
        check_vma=False,
    )
```

```python
import jax
import jax.numpy as jnp
from jax import lax
from jax.experimental import pallas as pl
from jax.experimental.pallas import tpu as pltpu
from jax.sharding import PartitionSpec as P

TILE = 16
NZ, NY, NX, NC = 8, 4, 4, 2
NDEV = 16
ROWS = 128
KG = 512
HID = 1792
CH = 128
NCH = HID // CH
NPAIR = NCH // 2
LAG = 2
GCOL = HID + 512
GHALF = GCOL // 2
GTICK = 6
EARLY_W = 4
RANK = 16
ADAPTERS = 16
AR = RANK * ADAPTERS
MESH = pl.DeviceIdType.MESH
NT = (((1,), (1,)), ((), ()))
F32 = jnp.float32
BF16 = jnp.bfloat16
OFFSETS = (0, 1, 7, 2, 6, 3, 5, 4)


def sigmoid(v):
    return 1.0 / (1.0 + jnp.exp(-v))


def kernel(
    g_any, w_any, gate_any, up_any, a_any, b_any, owner_ref, live_ref,
    hg_ref, og_ref,
    w_ref, a_ref, b_ref, gate_ref, up_ref, gsh,
    gs, gf, w2, hid, part, rbuf, sbuf, pg, rg, sg, sgf, grf, gsl, lo, lb, sel,
    ld, w_s, w_r, z_s, z_r, x_s, x_r, c_s, c_r, l_s, l_r,
    b_s, b_r, a_s, a_r, y_s, y_r,
):
    wa = lax.axis_index("wa")
    dev = lax.axis_index("dev")
    yh, z = lax.div(wa, NZ), lax.rem(wa, NZ)
    yl, low = lax.div(dev, 8), lax.rem(dev, 8)
    x, c = lax.div(low, 2), lax.rem(low, 2)
    sh = c * 4 + x

    far_dev = ((1 - yh) * NZ + z, dev)

    def z_device(off):
        return (yh * NZ + lax.rem(z + off, NZ), dev)

    def x_index(step):
        return lax.rem(x + step, NX)

    def x_device(step):
        return (wa, yl * 8 + x_index(step) * 2 + c)

    core_dev = (wa, yl * 8 + x * 2 + (1 - c))

    def dev_device(off):
        return (wa, lax.rem(dev + off, NDEV))

    def copy(src, dst, ssem, rsem, target):
        return pltpu.make_async_remote_copy(
            src_ref=src, dst_ref=dst, send_sem=ssem, recv_sem=rsem,
            device_id=target, device_id_type=MESH,
        )

    barrier = pltpu.get_barrier_semaphore()
    peers = [z_device(o) for o in (4, 3, 5, 2, 6, 1, 7)] + [far_dev]
    peers += [dev_device(o) for o in range(1, NDEV)]
    for peer in peers:
        pl.semaphore_signal(barrier, inc=1, device_id=peer, device_id_type=MESH)

    own_cols = pl.ds(pl.multiple_of(dev * KG, KG), KG)
    share_rows = pl.ds(pl.multiple_of(sh * TILE, TILE), TILE)
    loads = [
        pltpu.make_async_copy(src, dst, ld.at[i])
        for i, (src, dst) in enumerate(
            (
                (g_any.at[share_rows], gsh),
                (gate_any, gate_ref),
                (up_any, up_ref),
                (a_any, a_ref),
                (g_any.at[:, own_cols], gsl),
                (b_any, b_ref),
                (w_any, w_ref),
            )
        )
    ]
    for load in loads:
        load.start()

    live = live_ref[...].astype(F32)
    tile_lane = lax.broadcasted_iota(jnp.int32, (1, 128), 1)
    share_live = jnp.sum(
        jnp.where(tile_lane == wa * 8 + sh, live, 0.0), axis=1, keepdims=True
    )
    row16 = lax.broadcasted_iota(jnp.int32, (TILE, KG), 0).astype(F32)
    keep16 = row16 < share_live
    loads[0].wait()
    for q in range(NZ):
        for h in range(2):
            group = (yh if h == 0 else 1 - yh) * NZ + q
            cols = pl.ds(pl.multiple_of(group * KG, KG), KG)
            piece = jnp.where(keep16, gsh[:, cols], jnp.zeros((), BF16))
            gs[q, :, h * KG : (h + 1) * KG] = piece
    gf[pl.ds(z, 1), pl.ds(sh, 1)] = gs[pl.ds(z, 1)].reshape(1, 1, TILE, 2 * KG)

    def hidden_step(k, acc):
        cols = pl.ds(pl.multiple_of(k * 256, 256), 256)
        gate = gate_ref[:, cols].astype(F32)
        value = (gate * sigmoid(gate) * up_ref[:, cols].astype(F32)).astype(BF16)
        hid[:, cols] = value
        return acc + lax.dot_general(a_ref[:, cols], value, NT, preferred_element_type=F32)

    for i in (1, 2, 3):
        loads[i].wait()
    in_full = lax.fori_loop(0, HID // 256, hidden_step, jnp.zeros((AR, ROWS), F32))
    lane_tile = lax.broadcasted_iota(jnp.int32, (ROWS, 128), 1)
    sub_row = lax.broadcasted_iota(jnp.int32, (ROWS, 128), 0)
    pick = lane_tile == wa * 8 + lax.shift_right_logical(sub_row, 4)
    row_live = jnp.sum(jnp.where(pick, live, 0.0), axis=1, keepdims=True)
    position = lax.rem(lax.broadcasted_iota(jnp.int32, (ROWS, KG), 0), TILE).astype(F32)
    loads[4].wait()
    sliced = jnp.where(position < row_live, gsl[...], jnp.zeros((), BF16))
    gsl[...] = sliced
    loads[5].wait()
    out_full = lax.dot_general(b_ref[...], sliced, NT, preferred_element_type=F32)
    pick_t = sub_row == wa * 8 + lax.shift_right_logical(lane_tile, 4)
    owners = jnp.broadcast_to(owner_ref[...].astype(F32), (8, 128)).astype(BF16)
    chosen = jnp.where(pick_t, 1.0, 0.0).astype(BF16)
    owner_lane = jnp.dot(owners, chosen, preferred_element_type=F32)[0:1]
    adapter_row = lax.shift_right_logical(
        lax.broadcasted_iota(jnp.int32, (AR, ROWS), 0), 4
    ).astype(F32)
    selected = jnp.where(adapter_row == owner_lane, 1.0, 0.0)
    sel[...] = selected

    def choose(full):
        kept = jnp.where(selected > 0.5, full, 0.0)
        return jnp.sum(kept.reshape(ADAPTERS, RANK, ROWS), axis=0)

    lb[0, 0:RANK] = choose(in_full)
    lb[0, RANK : 2 * RANK] = choose(out_full)

    def l_copy(off):
        return copy(lb.at[0], lb.at[off], l_s.at[off], l_r.at[off], dev_device(off))

    def w_copy(j):
        rows = pl.ds(pl.multiple_of(j * 2 * CH, 2 * CH), 2 * CH)
        return copy(w_any.at[rows], w2.at[rows], w_s.at[j], w_r.at[j], far_dev)

    def z_send(off):
        zt = lax.rem(z + off, NZ)
        return copy(gs.at[zt], gf.at[z, sh], z_s.at[off], z_r.at[off], z_device(off))

    def source(q):
        return lax.rem(z + OFFSETS[q], NZ)

    def x_send(q, step):
        band = gf.at[source(q), sh]
        return copy(band, band, x_s.at[step, q], x_r.at[step, q], x_device(step))

    def x_recv(q, step):
        band = gf.at[source(q), c * 4 + x_index(NX - step)]
        return copy(band, band, x_s.at[step, q], x_r.at[step, q], x_device(step))

    def core_send(q):
        block = gf.at[source(q), pl.ds(c * 4, 4)]
        return copy(block, block, c_s.at[q], c_r.at[q], core_dev)

    def core_recv(q):
        block = gf.at[source(q), pl.ds((1 - c) * 4, 4)]
        return copy(block, block, c_s.at[q], c_r.at[q], core_dev)

    pl.semaphore_wait(barrier, len(peers))
    for off in (1, 7, 2, 6, 3, 5, 4):
        z_send(off).start()
    for j in range(EARLY_W):
        w_copy(j).start()
    for off in range(1, NDEV):
        l_copy(off).start()
    for q in range(NZ):
        if q > 0:
            off = NZ - OFFSETS[q]
            band = gf.at[source(q), sh]
            copy(band, band, z_s.at[off], z_r.at[off], z_device(off)).wait_recv()
        for step in (1, 3, 2):
            x_send(q, step).start()

    for off in range(1, NDEV):
        l_copy(off).wait_recv()
    total = jnp.zeros((2 * RANK, ROWS), F32)
    for src in range(NDEV):
        total = total + lb[lax.rem(dev + NDEV - src, NDEV)]
    summed = total.astype(BF16).astype(F32)
    keep = sel[...] > 0.5

    def spread(values):
        wide = jnp.broadcast_to(values[None], (ADAPTERS, RANK, ROWS)).reshape(AR, ROWS)
        return jnp.where(keep, wide, 0.0)

    spread_in = spread(summed[0:RANK]).astype(BF16)
    spread_out_wide = spread(summed[RANK : 2 * RANK])
    spread_out = spread_out_wide.astype(BF16)
    spread_out_t = spread_out_wide.T.astype(BF16)

    def adapter_step(k, carry):
        cols = pl.ds(pl.multiple_of(k * 256, 256), 256)
        grad = 2.0 * jnp.dot(spread_out, hid[:, cols], preferred_element_type=F32)
        pg[:, :, cols] = grad.reshape(ADAPTERS, RANK, 256)
        lo[:, cols] = 2.0 * jnp.dot(spread_out_t, a_ref[:, cols], preferred_element_type=F32)
        return carry

    lax.fori_loop(0, HID // 256, adapter_step, 0)
    grad_b = 2.0 * jnp.dot(spread_in, gsl[...], preferred_element_type=F32)
    pg[:, :, HID : HID + KG] = grad_b.reshape(ADAPTERS, RANK, KG)
    for q in range(NZ):
        sgf[q] = pg[(1 - yh) * NZ + q].astype(BF16)

    def adapter_exchange():
        return copy(sgf, grf, y_s, y_r, far_dev)

    adapter_exchange().start()
    for j in range(EARLY_W, NPAIR):
        w_copy(j).start()

    for q in range(NZ):
        for step in (1, 3, 2):
            x_recv(q, step).wait_recv()
        core_send(q).start()
    for q in range(NZ):
        core_recv(q).wait_recv()
    loads[6].wait()

    def z_next(d):
        return (yh * NZ + lax.rem(z + 1 + 6 * d, NZ), dev)

    def target_z(d, s):
        return lax.rem(z + NZ + (4 - s) * (1 - 2 * d), NZ)

    def b_copy(src, d, ch, s):
        return copy(src, rbuf.at[d, ch, s], b_s.at[d, ch, s], b_r.at[d, ch, s], z_next(d))

    def a_copy(src, d, k, s):
        return copy(src, rg.at[d, k, s], a_s.at[d, k, s], a_r.at[d, k, s], z_next(d))

    def base_first(ch, d, s):
        sbuf[ch, s] = part[ch, target_z(d, s)].astype(BF16)
        b_copy(sbuf.at[ch, s], d, ch, s).start()

    def base_forward(ch, d, s):
        slot = rbuf.at[d, ch, s - 1]
        b_copy(slot, d, ch, s - 1).wait_recv()
        slot[...] = (slot[...].astype(F32) + part[ch, target_z(d, s)]).astype(BF16)
        b_copy(slot, d, ch, s).start()

    def base_last(ch):
        for d in range(2):
            b_copy(rbuf.at[d, ch, 3], d, ch, 3).wait_recv()
        cols = pl.ds(pl.multiple_of(ch * CH, CH), CH)
        base = part[ch, z] + rbuf[0, ch, 3].astype(F32) + rbuf[1, ch, 3].astype(F32)
        hg_ref[:, cols] = base + lo[:, cols]

    def own_grads(k, zt):
        cols = slice(k * GHALF, (k + 1) * GHALF)
        return pg[yh * NZ + zt, :, cols] + grf[zt, :, cols].astype(F32)

    def adapter_first(k, d, s):
        sg[k, s] = own_grads(k, target_z(d, s)).astype(BF16)
        a_copy(sg.at[k, s], d, k, s).start()

    def adapter_forward(k, d, s):
        slot = rg.at[d, k, s - 1]
        a_copy(slot, d, k, s - 1).wait_recv()
        slot[...] = (slot[...].astype(F32) + own_grads(k, target_z(d, s))).astype(BF16)
        a_copy(slot, d, k, s).start()

    def adapter_last(k):
        for d in range(2):
            a_copy(rg.at[d, k, 3], d, k, 3).wait_recv()
        og_ref[:, k * GHALF : (k + 1) * GHALF] = (
            own_grads(k, z) + rg[0, k, 3].astype(F32) + rg[1, k, 3].astype(F32)
        )

    def product(j):
        rows = pl.ds(pl.multiple_of(j * 2 * CH, 2 * CH), 2 * CH)
        w_copy(j).wait_recv()
        mine = w_ref[rows, :]
        other = w2[rows, :]

        def block(k, carry):
            left = gf[pl.ds(2 * k, 2)].reshape(2 * ROWS, 2 * KG)
            value = lax.dot_general(left[:, :KG], mine, NT, preferred_element_type=F32)
            value = value + lax.dot_general(left[:, KG:], other, NT, preferred_element_type=F32)
            value = value.reshape(2, ROWS, 2 * CH)
            part[2 * j, pl.ds(2 * k, 2)] = value[:, :, :CH]
            part[2 * j + 1, pl.ds(2 * k, 2)] = value[:, :, CH:]
            return carry

        lax.fori_loop(0, NZ // 2, block, 0)

    def tick(t, carry):
        @pl.when((t < NCH) & (lax.rem(t, 2) == 0))
        def _():
            product(lax.div(t, 2))

        @pl.when(t < NCH)
        def _():
            base_first(t, lax.rem(t, 2), 0)

        for s in (1, 2, 3):
            ch = t - s * LAG

            @pl.when((ch >= 0) & (ch < NCH))
            def _(ch=ch, s=s):
                d4 = lax.rem(ch, 2)
                base_forward(ch, d4, s)
                if s == 1:
                    base_first(ch, 1 - d4, s)
                else:
                    base_forward(ch, 1 - d4, s)

        @pl.when(t == GTICK)
        def _():
            adapter_exchange().wait_recv()

        for k in range(2):
            @pl.when(t == GTICK + k)
            def _(k=k):
                adapter_first(k, k % 2, 0)

            for s in (1, 2, 3):
                @pl.when(t == GTICK + k + s * LAG)
                def _(k=k, s=s):
                    d4 = k % 2
                    adapter_forward(k, d4, s)
                    if s == 1:
                        adapter_first(k, 1 - d4, s)
                    else:
                        adapter_forward(k, 1 - d4, s)

            @pl.when(t == GTICK + k + 4 * LAG)
            def _(k=k):
                adapter_last(k)

        ch = t - 4 * LAG

        @pl.when(ch >= 0)
        def _():
            base_last(ch)

        return carry

    lax.fori_loop(0, NCH + 4 * LAG, tick, 0)

    adapter_exchange().wait_send()
    for off in range(1, NZ):
        z_send(off).wait_send()
    for off in range(1, NDEV):
        l_copy(off).wait_send()
    for q in range(NZ):
        for step in (1, 2, 3):
            x_send(q, step).wait_send()
        core_send(q).wait_send()
    for j in range(NPAIR):
        w_copy(j).wait_send()
    for k in range(2):
        for d in range(2):
            for s in range(4):
                if s > 0 or d == k % 2:
                    a_copy(rg.at[d, k, s], d, k, s).wait_send()

    def drain_b(ch, carry):
        d4 = lax.rem(ch, 2)
        b_copy(rbuf.at[d4, ch, 0], d4, ch, 0).wait_send()
        for d in range(2):
            for s in range(1, 4):
                b_copy(rbuf.at[d, ch, s], d, ch, s).wait_send()
        return carry

    lax.fori_loop(0, NCH, drain_b, 0)


def finish(hg_ref, og_ref, gate_ref, up_ref, ogate_ref, oup_ref, oga_ref, ogb_ref):
    oga_ref[...] = og_ref[:, :HID]
    ogb_ref[...] = og_ref[:, HID:]

    def step(k, carry):
        cols = pl.ds(pl.multiple_of(k * 256, 256), 256)
        grad = hg_ref[:, cols]
        gate = gate_ref[:, cols].astype(F32)
        up_value = up_ref[:, cols].astype(F32)
        s = sigmoid(gate)
        oup_ref[:, cols] = (grad * gate * s).astype(BF16)
        ogate_ref[:, cols] = (grad * up_value * s * (1.0 + gate * (1.0 - s))).astype(BF16)
        return carry

    lax.fori_loop(0, HID // 256, step, 0)


def on_device(grad, weight, gate, up, down_factor, up_factor, owner, live):
    dma = pltpu.SemaphoreType.DMA
    vmem = pltpu.VMEM
    whole = pl.BlockSpec(memory_space=pltpu.VMEM)
    anywhere = pl.BlockSpec(memory_space=pl.ANY)
    hidden_grad, adapter_grads = pl.pallas_call(
        kernel,
        out_shape=(
            jax.ShapeDtypeStruct((ROWS, HID), F32),
            jax.ShapeDtypeStruct((RANK, GCOL), F32),
        ),
        in_specs=[anywhere] * 6 + [whole] * 2,
        out_specs=(whole,) * 2,
        scratch_shapes=[
            vmem((HID, KG), BF16),
            vmem((AR, HID), BF16),
            vmem((AR, KG), BF16),
            vmem((ROWS, HID), BF16),
            vmem((ROWS, HID), BF16),
            vmem((TILE, 16 * KG), BF16),
            vmem((NZ, TILE, 2 * KG), BF16),
            vmem((NZ, 8, TILE, 2 * KG), BF16),
            vmem((HID, KG), BF16),
            vmem((ROWS, HID), BF16),
            vmem((NCH, NZ, ROWS, CH), F32),
            vmem((2, NCH, 4, ROWS, CH), BF16),
            vmem((NCH, 2, ROWS, CH), BF16),
            vmem((ADAPTERS, RANK, GCOL), F32),
            vmem((2, 2, 4, RANK, GHALF), BF16),
            vmem((2, 2, RANK, GHALF), BF16),
            vmem((NZ, RANK, GCOL), BF16),
            vmem((NZ, RANK, GCOL), BF16),
            vmem((ROWS, KG), BF16),
            vmem((ROWS, HID), F32),
            vmem((NDEV, 2 * RANK, ROWS), F32),
            vmem((AR, ROWS), F32),
            dma((7,)),
            dma((NPAIR,)), dma((NPAIR,)),
            dma((NZ,)), dma((NZ,)),
            dma((NX, NZ)), dma((NX, NZ)),
            dma((NZ,)), dma((NZ,)),
            dma((NDEV,)), dma((NDEV,)),
            dma((2, NCH, 4)), dma((2, NCH, 4)),
            dma((2, 2, 4)), dma((2, 2, 4)),
            dma, dma,
        ],
        compiler_params=pltpu.CompilerParams(
            collective_id=0, has_side_effects=True, vmem_limit_bytes=60 * 1024 * 1024
        ),
    )(
        grad, weight, gate, up,
        down_factor.reshape(AR, HID), up_factor.reshape(AR, KG),
        owner.reshape(1, owner.shape[0]), live.reshape(1, live.shape[0]),
    )
    out_gate, out_up, grad_a, grad_b = pl.pallas_call(
        finish,
        out_shape=(
            jax.ShapeDtypeStruct((ROWS, HID), BF16),
            jax.ShapeDtypeStruct((ROWS, HID), BF16),
            jax.ShapeDtypeStruct((RANK, HID), F32),
            jax.ShapeDtypeStruct((RANK, KG), F32),
        ),
        in_specs=[whole] * 4,
        out_specs=(whole,) * 4,
    )(hidden_grad, adapter_grads, gate, up)
    return out_gate, out_up, grad_a[None], grad_b[None]


def solution(mesh):
    placed = (
        P("wa", None),
        P("dev", "wa"),
        P("wa", "dev"),
        P("wa", "dev"),
        P(None, None, "dev"),
        P(None, None, "dev"),
        P(),
        P(),
    )
    return jax.shard_map(
        on_device,
        mesh=mesh,
        in_specs=placed,
        out_specs=(P("wa", "dev"), P("wa", "dev"), P("wa", None, "dev"), P("wa", None, "dev")),
        check_vma=False,
    )
```

```python
import jax
import jax.numpy as jnp
from jax import lax
from jax.experimental import pallas as pl
from jax.experimental.pallas import tpu as pltpu
from jax.sharding import PartitionSpec as P

TILE = 16
NZ, NY, NX, NC = 8, 4, 4, 2
NDEV = 16
ROWS = 128
KG = 512
HID = 1792
CH = 128
NCH = HID // CH
NPAIR = NCH // 2
LAG = 2
GCOL = HID + 512
GHALF = GCOL // 2
GTICK = 8
ATICK = 5
EARLY_W = 2
FH = HID // 2
GH = KG // 2
RANK = 16
ADAPTERS = 16
AR = RANK * ADAPTERS
MESH = pl.DeviceIdType.MESH
NT = (((1,), (1,)), ((), ()))
F32 = jnp.float32
BF16 = jnp.bfloat16
OFFSETS = (0, 1, 7, 2, 6, 3, 5, 4)


def sigmoid(v):
    return 1.0 / (1.0 + jnp.exp(-v))


def kernel(
    g_any, w_any, gate_any, up_any, a_any, b_any, owner_ref, live_ref,
    hg_ref, og_ref,
    w_ref, a_ref, b_ref, gate_ref, up_ref, gsh,
    gs, gf, w2, hid, part, rbuf, sbuf, pg, rg, sg, hs, hx, so, lx, tg, tb, gr, gsl, lo, lb, sel,
    ld, w_s, w_r, z_s, z_r, x_s, x_r, c_s, c_r, l_s, l_r,
    b_s, b_r, a_s, a_r, h_s, h_r, k_s, k_r, y_s, y_r,
):
    wa = lax.axis_index("wa")
    dev = lax.axis_index("dev")
    yh, z = lax.div(wa, NZ), lax.rem(wa, NZ)
    yl, low = lax.div(dev, 8), lax.rem(dev, 8)
    x, c = lax.div(low, 2), lax.rem(low, 2)
    sh = c * 4 + x

    far_dev = ((1 - yh) * NZ + z, dev)

    def z_device(off):
        return (yh * NZ + lax.rem(z + off, NZ), dev)

    def x_index(step):
        return lax.rem(x + step, NX)

    def x_device(step):
        return (wa, yl * 8 + x_index(step) * 2 + c)

    core_dev = (wa, yl * 8 + x * 2 + (1 - c))

    def dev_device(off):
        return (wa, lax.rem(dev + off, NDEV))

    def copy(src, dst, ssem, rsem, target):
        return pltpu.make_async_remote_copy(
            src_ref=src, dst_ref=dst, send_sem=ssem, recv_sem=rsem,
            device_id=target, device_id_type=MESH,
        )

    barrier = pltpu.get_barrier_semaphore()
    peers = [z_device(o) for o in (4, 3, 5, 2, 6, 1, 7)] + [far_dev]
    peers += [dev_device(o) for o in range(1, NDEV)]
    for peer in peers:
        pl.semaphore_signal(barrier, inc=1, device_id=peer, device_id_type=MESH)

    own_cols = pl.ds(pl.multiple_of(dev * KG, KG), KG)
    share_rows = pl.ds(pl.multiple_of(sh * TILE, TILE), TILE)
    loads = [
        pltpu.make_async_copy(src, dst, ld.at[i])
        for i, (src, dst) in enumerate(
            (
                (g_any.at[share_rows], gsh),
                (gate_any, gate_ref),
                (up_any, up_ref),
                (a_any, a_ref),
                (g_any.at[:, own_cols], gsl),
                (b_any, b_ref),
                (w_any, w_ref),
            )
        )
    ]
    for load in loads:
        load.start()

    live = live_ref[...].astype(F32)
    tile_lane = lax.broadcasted_iota(jnp.int32, (1, 128), 1)
    share_live = jnp.sum(
        jnp.where(tile_lane == wa * 8 + sh, live, 0.0), axis=1, keepdims=True
    )
    row16 = lax.broadcasted_iota(jnp.int32, (TILE, KG), 0).astype(F32)
    keep16 = row16 < share_live
    loads[0].wait()
    for q in range(NZ):
        for h in range(2):
            group = (yh if h == 0 else 1 - yh) * NZ + q
            cols = pl.ds(pl.multiple_of(group * KG, KG), KG)
            piece = jnp.where(keep16, gsh[:, cols], jnp.zeros((), BF16))
            gs[q, :, h * KG : (h + 1) * KG] = piece
    gf[pl.ds(z, 1), pl.ds(sh, 1)] = gs[pl.ds(z, 1)].reshape(1, 1, TILE, 2 * KG)

    def hidden_step(k, acc):
        cols = pl.ds(pl.multiple_of(k * 256, 256), 256)
        gate = gate_ref[:, cols].astype(F32)
        value = (gate * sigmoid(gate) * up_ref[:, cols].astype(F32)).astype(BF16)
        hid[:, cols] = value
        return acc + lax.dot_general(a_ref[:, cols], value, NT, preferred_element_type=F32)

    for i in (1, 2, 3):
        loads[i].wait()
    in_full = lax.fori_loop(0, HID // 256, hidden_step, jnp.zeros((AR, ROWS), F32))
    lane_tile = lax.broadcasted_iota(jnp.int32, (ROWS, 128), 1)
    sub_row = lax.broadcasted_iota(jnp.int32, (ROWS, 128), 0)
    pick = lane_tile == wa * 8 + lax.shift_right_logical(sub_row, 4)
    row_live = jnp.sum(jnp.where(pick, live, 0.0), axis=1, keepdims=True)
    position = lax.rem(lax.broadcasted_iota(jnp.int32, (ROWS, KG), 0), TILE).astype(F32)
    loads[4].wait()
    sliced = jnp.where(position < row_live, gsl[...], jnp.zeros((), BF16))
    gsl[...] = sliced
    loads[5].wait()
    out_full = lax.dot_general(b_ref[...], sliced, NT, preferred_element_type=F32)
    far_half = 1 - yh
    hs[:, :FH] = hid[:, pl.ds(pl.multiple_of(far_half * FH, 128), FH)]
    hs[:, FH:] = gsl[:, pl.ds(pl.multiple_of(far_half * GH, 128), GH)]
    hx[0, :, :FH] = hid[:, pl.ds(pl.multiple_of(yh * FH, 128), FH)]
    hx[0, :, FH:] = gsl[:, pl.ds(pl.multiple_of(yh * GH, 128), GH)]
    owners = jnp.broadcast_to(owner_ref[...].astype(F32), (8, 128)).astype(BF16)
    adapter_row = lax.shift_right_logical(
        lax.broadcasted_iota(jnp.int32, (AR, ROWS), 0), 4
    ).astype(F32)

    def select(group):
        pick_t = sub_row == group * 8 + lax.shift_right_logical(lane_tile, 4)
        chosen = jnp.where(pick_t, 1.0, 0.0).astype(BF16)
        owner_lane = jnp.dot(owners, chosen, preferred_element_type=F32)[0:1]
        return jnp.where(adapter_row == owner_lane, 1.0, 0.0)

    selected = select(wa)
    sel[0] = selected
    sel[1] = select(far_half * NZ + z)

    def choose(full):
        kept = jnp.where(selected > 0.5, full, 0.0)
        return jnp.sum(kept.reshape(ADAPTERS, RANK, ROWS), axis=0)

    lb[0, 0:RANK] = choose(in_full)
    lb[0, RANK : 2 * RANK] = choose(out_full)

    def l_copy(off):
        return copy(lb.at[0], lb.at[off], l_s, l_r.at[off], dev_device(off))

    def w_copy(j):
        rows = pl.ds(pl.multiple_of(j * 2 * CH, 2 * CH), 2 * CH)
        return copy(w_any.at[rows], w2.at[rows], w_s, w_r.at[j], far_dev)

    def z_send(off):
        zt = lax.rem(z + off, NZ)
        return copy(gs.at[zt], gf.at[z, sh], z_s, z_r.at[off], z_device(off))

    def source(q):
        return lax.rem(z + OFFSETS[q], NZ)

    def x_send(q, step):
        band = gf.at[source(q), sh]
        return copy(band, band, x_s, x_r.at[step, q], x_device(step))

    def x_recv(q, step):
        band = gf.at[source(q), c * 4 + x_index(NX - step)]
        return copy(band, band, x_s, x_r.at[step, q], x_device(step))

    def core_send(q):
        block = gf.at[source(q), pl.ds(c * 4, 4)]
        return copy(block, block, c_s, c_r.at[q], core_dev)

    def core_recv(q):
        block = gf.at[source(q), pl.ds((1 - c) * 4, 4)]
        return copy(block, block, c_s, c_r.at[q], core_dev)

    pl.semaphore_wait(barrier, len(peers))
    for off in (1, 7, 2, 6, 3, 5, 4):
        z_send(off).start()
    for off in range(1, NDEV):
        l_copy(off).start()
    for j in range(EARLY_W):
        w_copy(j).start()
    for q in range(NZ):
        if q > 0:
            off = NZ - OFFSETS[q]
            band = gf.at[source(q), sh]
            copy(band, band, z_s, z_r.at[off], z_device(off)).wait_recv()
        for step in (1, 3, 2):
            x_send(q, step).start()

    for off in range(1, NDEV):
        l_copy(off).wait_recv()
    total = jnp.zeros((2 * RANK, ROWS), F32)
    for src in range(NDEV):
        total = total + lb[lax.rem(dev + NDEV - src, NDEV)]
    lx[0] = total.astype(BF16)

    def sums_copy():
        return copy(lx.at[0], lx.at[1], k_s, k_r, far_dev)

    def half_copy():
        return copy(hs, hx.at[1], h_s, h_r, far_dev)

    sums_copy().start()
    half_copy().start()

    def spread(which, first):
        values = lx[which, first : first + RANK].astype(F32)
        wide = jnp.broadcast_to(values[None], (ADAPTERS, RANK, ROWS)).reshape(AR, ROWS)
        return jnp.where(sel[which] > 0.5, wide, 0.0)

    spread_out_wide = spread(0, RANK)
    so[0, :, :ROWS] = spread(0, 0).astype(BF16)
    so[1, :, :ROWS] = spread_out_wide.astype(BF16)
    spread_out_t = spread_out_wide.T.astype(BF16)

    def adapter_step(k, carry):
        cols = pl.ds(pl.multiple_of(k * 256, 256), 256)
        lo[:, cols] = 2.0 * jnp.dot(spread_out_t, a_ref[:, cols], preferred_element_type=F32)
        return carry

    lax.fori_loop(0, HID // 256, adapter_step, 0)

    def adapter_grads():
        sums_copy().wait_recv()
        half_copy().wait_recv()
        so[0, :, ROWS:] = spread(1, 0).astype(BF16)
        so[1, :, ROWS:] = spread(1, RANK).astype(BF16)

        def columns(which, cols, width):
            left = jnp.concatenate([hx[0, :, cols], hx[1, :, cols]], axis=0)
            grad = 2.0 * jnp.dot(so[which], left, preferred_element_type=F32)
            pg[:, :, cols] = grad.reshape(ADAPTERS, RANK, width)

        def grad_step(k, carry):
            columns(1, pl.ds(pl.multiple_of(k * 128, 128), 128), 128)
            return carry

        lax.fori_loop(0, FH // 128, grad_step, 0)
        columns(0, slice(FH, FH + GH), GH)

    for q in range(NZ):
        for step in (1, 3, 2):
            x_recv(q, step).wait_recv()
        core_send(q).start()
    for q in range(NZ):
        core_recv(q).wait_recv()
    loads[6].wait()

    def z_next(d):
        return (yh * NZ + lax.rem(z + 1 + 6 * d, NZ), dev)

    def target_z(d, s):
        return lax.rem(z + NZ + (4 - s) * (1 - 2 * d), NZ)

    def b_copy(src, d, ch, s):
        return copy(src, rbuf.at[d, ch, s], b_s, b_r.at[d, ch, s], z_next(d))

    def a_copy(src, d, k, s):
        return copy(src, rg.at[d, k, s], a_s.at[d, k, s], a_r.at[d, k, s], z_next(d))

    def base_first(ch, d, s):
        sbuf[ch, s] = part[ch, target_z(d, s)].astype(BF16)
        b_copy(sbuf.at[ch, s], d, ch, s).start()

    def base_forward(ch, d, s):
        slot = rbuf.at[d, ch, s - 1]
        b_copy(slot, d, ch, s - 1).wait_recv()
        slot[...] = (slot[...].astype(F32) + part[ch, target_z(d, s)]).astype(BF16)
        b_copy(slot, d, ch, s).start()

    def base_last(ch):
        for d in range(2):
            b_copy(rbuf.at[d, ch, 3], d, ch, 3).wait_recv()
        cols = pl.ds(pl.multiple_of(ch * CH, CH), CH)
        base = part[ch, z] + rbuf[0, ch, 3].astype(F32) + rbuf[1, ch, 3].astype(F32)
        hg_ref[:, cols] = base + lo[:, cols]

    def own_grads(k, zt):
        return pg[k * NZ + zt]

    def far_grads():
        return copy(tb.at[far_half], gr, y_s, y_r, far_dev)

    def adapter_first(k, d, s):
        sg[k, s] = own_grads(k, target_z(d, s)).astype(BF16)
        a_copy(sg.at[k, s], d, k, s).start()

    def adapter_forward(k, d, s):
        slot = rg.at[d, k, s - 1]
        a_copy(slot, d, k, s - 1).wait_recv()
        slot[...] = (slot[...].astype(F32) + own_grads(k, target_z(d, s))).astype(BF16)
        a_copy(slot, d, k, s).start()

    def adapter_last(k):
        for d in range(2):
            a_copy(rg.at[d, k, 3], d, k, 3).wait_recv()
        done = own_grads(k, z) + rg[0, k, 3].astype(F32) + rg[1, k, 3].astype(F32)
        tg[k] = done
        tb[k] = done.astype(BF16)

    def product(j):
        rows = pl.ds(pl.multiple_of(j * 2 * CH, 2 * CH), 2 * CH)
        w_copy(j).wait_recv()
        mine = w_ref[rows, :]
        other = w2[rows, :]

        def block(k, carry):
            left = gf[pl.ds(2 * k, 2)].reshape(2 * ROWS, 2 * KG)
            value = lax.dot_general(left[:, :KG], mine, NT, preferred_element_type=F32)
            value = value + lax.dot_general(left[:, KG:], other, NT, preferred_element_type=F32)
            value = value.reshape(2, ROWS, 2 * CH)
            part[2 * j, pl.ds(2 * k, 2)] = value[:, :, :CH]
            part[2 * j + 1, pl.ds(2 * k, 2)] = value[:, :, CH:]
            return carry

        lax.fori_loop(0, NZ // 2, block, 0)

    def tick(t, carry):
        @pl.when((t < NCH) & (lax.rem(t, 2) == 0))
        def _():
            @pl.when(lax.div(t, 2) + EARLY_W < NPAIR)
            def _():
                w_copy(lax.div(t, 2) + EARLY_W).start()

            product(lax.div(t, 2))

        @pl.when(t < NCH)
        def _():
            base_first(t, lax.rem(t, 2), 0)

        for s in (1, 2, 3):
            ch = t - s * LAG

            @pl.when((ch >= 0) & (ch < NCH))
            def _(ch=ch, s=s):
                d4 = lax.rem(ch, 2)
                base_forward(ch, d4, s)
                if s == 1:
                    base_first(ch, 1 - d4, s)
                else:
                    base_forward(ch, 1 - d4, s)

        @pl.when(t == ATICK)
        def _():
            adapter_grads()

        for k in range(2):
            @pl.when(t == GTICK + k)
            def _(k=k):
                adapter_first(k, k % 2, 0)

            for s in (1, 2, 3):
                @pl.when(t == GTICK + k + s * LAG)
                def _(k=k, s=s):
                    d4 = k % 2
                    adapter_forward(k, d4, s)
                    if s == 1:
                        adapter_first(k, 1 - d4, s)
                    else:
                        adapter_forward(k, 1 - d4, s)

            @pl.when(t == GTICK + k + 4 * LAG)
            def _(k=k):
                adapter_last(k)

        @pl.when(t == GTICK + 2 + 4 * LAG)
        def _():
            far_grads().start()

        ch = t - 4 * LAG

        @pl.when(ch >= 0)
        def _():
            base_last(ch)

        return carry

    lax.fori_loop(0, NCH + 4 * LAG, tick, 0)

    far_grads().wait_recv()
    og_ref[pl.ds(yh, 1)] = tg[pl.ds(yh, 1)]
    og_ref[pl.ds(far_half, 1)] = gr[...].astype(F32)[None]

    def sent(block, sem):
        copy(block, block, sem, k_r, far_dev).wait_send()

    far_grads().wait_send()
    sums_copy().wait_send()
    half_copy().wait_send()
    sent(gf.at[0, 0 : NZ - 1], z_s)
    sent(lb.at[1:NDEV], l_s)
    sent(gf.at[0 : NX - 1], x_s)
    sent(gf.at[0 : NZ // 2], c_s)
    sent(w2, w_s)
    for k in range(2):
        for d in range(2):
            for s in range(4):
                if s > 0 or d == k % 2:
                    a_copy(rg.at[d, k, s], d, k, s).wait_send()
    sent(part.at[0 : NCH // 2, 0 : NZ - 1], b_s)


def finish(hg_ref, og_ref, gate_ref, up_ref, ogate_ref, oup_ref, oga_ref, ogb_ref):
    for h in range(2):
        oga_ref[:, h * FH : (h + 1) * FH] = og_ref[h, :, :FH]
        ogb_ref[:, h * GH : (h + 1) * GH] = og_ref[h, :, FH:]

    def step(k, carry):
        cols = pl.ds(pl.multiple_of(k * 256, 256), 256)
        grad = hg_ref[:, cols]
        gate = gate_ref[:, cols].astype(F32)
        up_value = up_ref[:, cols].astype(F32)
        s = sigmoid(gate)
        oup_ref[:, cols] = (grad * gate * s).astype(BF16)
        ogate_ref[:, cols] = (grad * up_value * s * (1.0 + gate * (1.0 - s))).astype(BF16)
        return carry

    lax.fori_loop(0, HID // 256, step, 0)


def on_device(grad, weight, gate, up, down_factor, up_factor, owner, live):
    dma = pltpu.SemaphoreType.DMA
    vmem = pltpu.VMEM
    whole = pl.BlockSpec(memory_space=pltpu.VMEM)
    anywhere = pl.BlockSpec(memory_space=pl.ANY)
    hidden_grad, adapter_grads = pl.pallas_call(
        kernel,
        out_shape=(
            jax.ShapeDtypeStruct((ROWS, HID), F32),
            jax.ShapeDtypeStruct((2, RANK, GHALF), F32),
        ),
        in_specs=[anywhere] * 6 + [whole] * 2,
        out_specs=(whole,) * 2,
        scratch_shapes=[
            vmem((HID, KG), BF16),
            vmem((AR, HID), BF16),
            vmem((AR, KG), BF16),
            vmem((ROWS, HID), BF16),
            vmem((ROWS, HID), BF16),
            vmem((TILE, 16 * KG), BF16),
            vmem((NZ, TILE, 2 * KG), BF16),
            vmem((NZ, 8, TILE, 2 * KG), BF16),
            vmem((HID, KG), BF16),
            vmem((ROWS, HID), BF16),
            vmem((NCH, NZ, ROWS, CH), F32),
            vmem((2, NCH, 4, ROWS, CH), BF16),
            vmem((NCH, 2, ROWS, CH), BF16),
            vmem((ADAPTERS, RANK, GHALF), F32),
            vmem((2, 2, 4, RANK, GHALF), BF16),
            vmem((2, 2, RANK, GHALF), BF16),
            vmem((ROWS, GHALF), BF16),
            vmem((2, ROWS, GHALF), BF16),
            vmem((2, AR, 2 * ROWS), BF16),
            vmem((2, 2 * RANK, ROWS), BF16),
            vmem((2, RANK, GHALF), F32),
            vmem((2, RANK, GHALF), BF16),
            vmem((RANK, GHALF), BF16),
            vmem((ROWS, KG), BF16),
            vmem((ROWS, HID), F32),
            vmem((NDEV, 2 * RANK, ROWS), F32),
            vmem((2, AR, ROWS), F32),
            dma((7,)),
            dma, dma((NPAIR,)),
            dma, dma((NZ,)),
            dma, dma((NX, NZ)),
            dma, dma((NZ,)),
            dma, dma((NDEV,)),
            dma, dma((2, NCH, 4)),
            dma((2, 2, 4)), dma((2, 2, 4)),
            dma, dma,
            dma, dma,
            dma, dma,
        ],
        compiler_params=pltpu.CompilerParams(
            collective_id=0, has_side_effects=True, vmem_limit_bytes=60 * 1024 * 1024
        ),
    )(
        grad, weight, gate, up,
        down_factor.reshape(AR, HID), up_factor.reshape(AR, KG),
        owner.reshape(1, owner.shape[0]), live.reshape(1, live.shape[0]),
    )
    out_gate, out_up, grad_a, grad_b = pl.pallas_call(
        finish,
        out_shape=(
            jax.ShapeDtypeStruct((ROWS, HID), BF16),
            jax.ShapeDtypeStruct((ROWS, HID), BF16),
            jax.ShapeDtypeStruct((RANK, HID), F32),
            jax.ShapeDtypeStruct((RANK, KG), F32),
        ),
        in_specs=[whole] * 4,
        out_specs=(whole,) * 4,
    )(hidden_grad, adapter_grads, gate, up)
    return out_gate, out_up, grad_a[None], grad_b[None]


def solution(mesh):
    placed = (
        P("wa", None),
        P("dev", "wa"),
        P("wa", "dev"),
        P("wa", "dev"),
        P(None, None, "dev"),
        P(None, None, "dev"),
        P(),
        P(),
    )
    return jax.shard_map(
        on_device,
        mesh=mesh,
        in_specs=placed,
        out_specs=(P("wa", "dev"), P("wa", "dev"), P("wa", None, "dev"), P("wa", None, "dev")),
        check_vma=False,
    )
```

```python
import jax
import jax.numpy as jnp
from jax import lax
from jax.experimental import pallas as pl
from jax.experimental.pallas import tpu as pltpu
from jax.sharding import PartitionSpec as P

TILE = 16
NZ, NY, NX, NC = 8, 4, 4, 2
NDEV = 16
ROWS = 128
KG = 512
HID = 1792
CH = 128
NCH = HID // CH
NPAIR = NCH // 2
GCOL = HID + 512
GHALF = GCOL // 2
GITEM = 2
ITEMS = NPAIR + 1
EARLY_W = 3
FH = HID // 2
GH = KG // 2
RANK = 16
ADAPTERS = 16
AR = RANK * ADAPTERS
MESH = pl.DeviceIdType.MESH
NT = (((1,), (1,)), ((), ()))
F32 = jnp.float32
BF16 = jnp.bfloat16
OFFSETS = (0, 1, 7, 2, 6, 3, 5, 4)


def sigmoid(v):
    return 1.0 / (1.0 + jnp.exp(-v))


def kernel(
    g_any, w_any, gate_any, up_any, a_any, b_any, owner_ref, live_ref,
    hg_ref, og_ref,
    w_ref, a_ref, b_ref, gate_ref, up_ref, gsh,
    gs, gf, w2, hid, part, rbuf, sbuf, pg, rg, sg, hs, hx, so, lx, tg, tb, gr, gsl, lo, lb, ls, sel,
    ld, w_s, w_r, z_s, z_r, x_s, x_r, c_s, c_r, l_s, l_r, t_s, t_r,
    b_s, b_r, a_s, a_r, h_s, h_r, k_s, k_r, y_s, y_r,
):
    wa = lax.axis_index("wa")
    dev = lax.axis_index("dev")
    yh, z = lax.div(wa, NZ), lax.rem(wa, NZ)
    yl, low = lax.div(dev, 8), lax.rem(dev, 8)
    x, c = lax.div(low, 2), lax.rem(low, 2)
    sh = c * 4 + x

    far_dev = ((1 - yh) * NZ + z, dev)

    def z_device(off):
        return (yh * NZ + lax.rem(z + off, NZ), dev)

    def x_index(step):
        return lax.rem(x + step, NX)

    def x_device(step):
        return (wa, yl * 8 + x_index(step) * 2 + c)

    core_dev = (wa, yl * 8 + x * 2 + (1 - c))

    def low_device(off):
        return (wa, yl * 8 + lax.rem(low + off, 8))

    side_dev = (wa, lax.rem(dev + 8, NDEV))

    def copy(src, dst, ssem, rsem, target):
        return pltpu.make_async_remote_copy(
            src_ref=src, dst_ref=dst, send_sem=ssem, recv_sem=rsem,
            device_id=target, device_id_type=MESH,
        )

    barrier = pltpu.get_barrier_semaphore()
    peers = [z_device(o) for o in (4, 3, 5, 2, 6, 1, 7)] + [far_dev, side_dev]
    peers += [low_device(o) for o in range(1, 8)]
    for peer in peers:
        pl.semaphore_signal(barrier, inc=1, device_id=peer, device_id_type=MESH)

    own_cols = pl.ds(pl.multiple_of(dev * KG, KG), KG)
    share_rows = pl.ds(pl.multiple_of(sh * TILE, TILE), TILE)
    loads = [
        pltpu.make_async_copy(src, dst, ld.at[i])
        for i, (src, dst) in enumerate(
            (
                (g_any.at[share_rows], gsh),
                (gate_any, gate_ref),
                (up_any, up_ref),
                (a_any, a_ref),
                (g_any.at[:, own_cols], gsl),
                (b_any, b_ref),
                (w_any, w_ref),
            )
        )
    ]
    for load in loads:
        load.start()

    live = live_ref[...].astype(F32)
    tile_lane = lax.broadcasted_iota(jnp.int32, (1, 128), 1)
    share_live = jnp.sum(
        jnp.where(tile_lane == wa * 8 + sh, live, 0.0), axis=1, keepdims=True
    )
    row16 = lax.broadcasted_iota(jnp.int32, (TILE, KG), 0).astype(F32)
    keep16 = row16 < share_live
    loads[0].wait()
    for q in range(NZ):
        for h in range(2):
            group = (yh if h == 0 else 1 - yh) * NZ + q
            cols = pl.ds(pl.multiple_of(group * KG, KG), KG)
            piece = jnp.where(keep16, gsh[:, cols], jnp.zeros((), BF16))
            gs[q, :, h * KG : (h + 1) * KG] = piece
    gf[pl.ds(z, 1), pl.ds(sh, 1)] = gs[pl.ds(z, 1)].reshape(1, 1, TILE, 2 * KG)

    def hidden_step(k, acc):
        cols = pl.ds(pl.multiple_of(k * 256, 256), 256)
        gate = gate_ref[:, cols].astype(F32)
        value = (gate * sigmoid(gate) * up_ref[:, cols].astype(F32)).astype(BF16)
        hid[:, cols] = value
        return acc + lax.dot_general(a_ref[:, cols], value, NT, preferred_element_type=F32)

    for i in (1, 2, 3):
        loads[i].wait()
    in_full = lax.fori_loop(0, HID // 256, hidden_step, jnp.zeros((AR, ROWS), F32))
    lane_tile = lax.broadcasted_iota(jnp.int32, (ROWS, 128), 1)
    sub_row = lax.broadcasted_iota(jnp.int32, (ROWS, 128), 0)
    pick = lane_tile == wa * 8 + lax.shift_right_logical(sub_row, 4)
    row_live = jnp.sum(jnp.where(pick, live, 0.0), axis=1, keepdims=True)
    position = lax.rem(lax.broadcasted_iota(jnp.int32, (ROWS, KG), 0), TILE).astype(F32)
    loads[4].wait()
    sliced = jnp.where(position < row_live, gsl[...], jnp.zeros((), BF16))
    gsl[...] = sliced
    loads[5].wait()
    out_full = lax.dot_general(b_ref[...], sliced, NT, preferred_element_type=F32)
    far_half = 1 - yh
    hs[:, :FH] = hid[:, pl.ds(pl.multiple_of(far_half * FH, 128), FH)]
    hs[:, FH:] = gsl[:, pl.ds(pl.multiple_of(far_half * GH, 128), GH)]
    hx[0, :, :FH] = hid[:, pl.ds(pl.multiple_of(yh * FH, 128), FH)]
    hx[0, :, FH:] = gsl[:, pl.ds(pl.multiple_of(yh * GH, 128), GH)]
    owners = jnp.broadcast_to(owner_ref[...].astype(F32), (8, 128)).astype(BF16)
    adapter_row = lax.shift_right_logical(
        lax.broadcasted_iota(jnp.int32, (AR, ROWS), 0), 4
    ).astype(F32)

    def select(group):
        pick_t = sub_row == group * 8 + lax.shift_right_logical(lane_tile, 4)
        chosen = jnp.where(pick_t, 1.0, 0.0).astype(BF16)
        owner_lane = jnp.dot(owners, chosen, preferred_element_type=F32)[0:1]
        return jnp.where(adapter_row == owner_lane, 1.0, 0.0)

    selected = select(wa)
    sel[0] = selected
    sel[1] = select(far_half * NZ + z)

    def choose(full):
        kept = jnp.where(selected > 0.5, full, 0.0)
        return jnp.sum(kept.reshape(ADAPTERS, RANK, ROWS), axis=0)

    lb[0, 0:RANK] = choose(in_full)
    lb[0, RANK : 2 * RANK] = choose(out_full)

    def l_copy(off):
        return copy(lb.at[0], lb.at[off], l_s, l_r.at[off], low_device(off))

    def w_copy(j):
        rows = pl.ds(pl.multiple_of(j * 2 * CH, 2 * CH), 2 * CH)
        return copy(w_any.at[rows], w2.at[rows], w_s, w_r.at[j], far_dev)

    def z_send(off):
        zt = lax.rem(z + off, NZ)
        return copy(gs.at[zt], gf.at[z, sh], z_s, z_r.at[off], z_device(off))

    def source(q):
        return lax.rem(z + OFFSETS[q], NZ)

    def x_send(q, step):
        band = gf.at[source(q), sh]
        return copy(band, band, x_s, x_r.at[step, q], x_device(step))

    def x_recv(q, step):
        band = gf.at[source(q), c * 4 + x_index(NX - step)]
        return copy(band, band, x_s, x_r.at[step, q], x_device(step))

    def core_send(q):
        block = gf.at[source(q), pl.ds(c * 4, 4)]
        return copy(block, block, c_s, c_r.at[q], core_dev)

    def core_recv(q):
        block = gf.at[source(q), pl.ds((1 - c) * 4, 4)]
        return copy(block, block, c_s, c_r.at[q], core_dev)

    pl.semaphore_wait(barrier, len(peers))
    for off in (1, 7, 2, 6, 3, 5, 4):
        z_send(off).start()
    for off in range(1, 8):
        l_copy(off).start()
    w_copy(0).start()

    def side_copy():
        return copy(ls.at[0], ls.at[1], t_s, t_r, side_dev)

    for q in range(NZ):
        if q > 0:
            off = NZ - OFFSETS[q]
            band = gf.at[source(q), sh]
            copy(band, band, z_s, z_r.at[off], z_device(off)).wait_recv()
        for step in (1, 3, 2):
            x_send(q, step).start()
        if q == 2:
            for off in range(1, 8):
                l_copy(off).wait_recv()
            part_sum = jnp.zeros((2 * RANK, ROWS), F32)
            for src in range(8):
                part_sum = part_sum + lb[lax.rem(low + 8 - src, 8)]
            ls[0] = part_sum
            side_copy().start()
            w_copy(1).start()

    side_copy().wait_recv()
    total = ls[0] + ls[1]
    lx[0] = total.astype(BF16)

    def sums_copy():
        return copy(lx.at[0], lx.at[1], k_s, k_r, far_dev)

    def half_copy():
        return copy(hs, hx.at[1], h_s, h_r, far_dev)

    sums_copy().start()
    half_copy().start()
    for j in range(2, EARLY_W):
        w_copy(j).start()

    def spread(which, first):
        values = lx[which, first : first + RANK].astype(F32)
        wide = jnp.broadcast_to(values[None], (ADAPTERS, RANK, ROWS)).reshape(AR, ROWS)
        return jnp.where(sel[which] > 0.5, wide, 0.0)

    spread_out_wide = spread(0, RANK)
    so[0, :, :ROWS] = spread(0, 0).astype(BF16)
    so[1, :, :ROWS] = spread_out_wide.astype(BF16)
    spread_out_t = spread_out_wide.T.astype(BF16)

    def adapter_step(k, carry):
        cols = pl.ds(pl.multiple_of(k * 256, 256), 256)
        lo[:, cols] = 2.0 * jnp.dot(spread_out_t, a_ref[:, cols], preferred_element_type=F32)
        return carry

    lax.fori_loop(0, HID // 256, adapter_step, 0)

    def adapter_grads():
        sums_copy().wait_recv()
        half_copy().wait_recv()
        so[0, :, ROWS:] = spread(1, 0).astype(BF16)
        so[1, :, ROWS:] = spread(1, RANK).astype(BF16)

        def columns(which, cols, width):
            left = jnp.concatenate([hx[0, :, cols], hx[1, :, cols]], axis=0)
            grad = 2.0 * jnp.dot(so[which], left, preferred_element_type=F32)
            pg[:, :, cols] = grad.reshape(ADAPTERS, RANK, width)

        def grad_step(k, carry):
            columns(1, pl.ds(pl.multiple_of(k * 128, 128), 128), 128)
            return carry

        lax.fori_loop(0, FH // 128, grad_step, 0)
        columns(0, slice(FH, FH + GH), GH)

    for q in range(NZ):
        for step in (1, 3, 2):
            x_recv(q, step).wait_recv()
        core_send(q).start()
    for q in range(NZ):
        core_recv(q).wait_recv()
    loads[6].wait()

    def z_next(d):
        return (yh * NZ + lax.rem(z + 1 + 6 * d, NZ), dev)

    def target_z(d, s):
        return lax.rem(z + NZ + (4 - s) * (1 - 2 * d), NZ)

    def b_copy(src, d, ch, s):
        return copy(src, rbuf.at[d, ch, s], b_s, b_r.at[d, ch, s], z_next(d))

    def a_copy(src, d, k, s):
        return copy(src, rg.at[d, k, s], a_s.at[d, k, s], a_r.at[d, k, s], z_next(d))

    def base_first(ch, d, s):
        sbuf[ch, s] = part[ch, target_z(d, s)].astype(BF16)
        b_copy(sbuf.at[ch, s], d, ch, s).start()

    def base_forward(ch, d, s):
        slot = rbuf.at[d, ch, s - 1]
        b_copy(slot, d, ch, s - 1).wait_recv()
        slot[...] = (slot[...].astype(F32) + part[ch, target_z(d, s)]).astype(BF16)
        b_copy(slot, d, ch, s).start()

    def base_last(ch):
        for d in range(2):
            b_copy(rbuf.at[d, ch, 3], d, ch, 3).wait_recv()
        cols = pl.ds(pl.multiple_of(ch * CH, CH), CH)
        base = part[ch, z] + rbuf[0, ch, 3].astype(F32) + rbuf[1, ch, 3].astype(F32)
        hg_ref[:, cols] = base + lo[:, cols]

    def own_grads(k, zt):
        return pg[k * NZ + zt]

    def far_grads():
        return copy(tb.at[far_half], gr, y_s, y_r, far_dev)

    def adapter_first(k, d, s):
        sg[k, s] = own_grads(k, target_z(d, s)).astype(BF16)
        a_copy(sg.at[k, s], d, k, s).start()

    def adapter_forward(k, d, s):
        slot = rg.at[d, k, s - 1]
        a_copy(slot, d, k, s - 1).wait_recv()
        slot[...] = (slot[...].astype(F32) + own_grads(k, target_z(d, s))).astype(BF16)
        a_copy(slot, d, k, s).start()

    def adapter_last(k):
        for d in range(2):
            a_copy(rg.at[d, k, 3], d, k, 3).wait_recv()
        done = own_grads(k, z) + rg[0, k, 3].astype(F32) + rg[1, k, 3].astype(F32)
        tg[k] = done
        tb[k] = done.astype(BF16)

    def product(j):
        rows = pl.ds(pl.multiple_of(j * 2 * CH, 2 * CH), 2 * CH)
        w_copy(j).wait_recv()
        mine = w_ref[rows, :]
        other = w2[rows, :]

        def block(k, carry):
            left = gf[pl.ds(2 * k, 2)].reshape(2 * ROWS, 2 * KG)
            value = lax.dot_general(left[:, :KG], mine, NT, preferred_element_type=F32)
            value = value + lax.dot_general(left[:, KG:], other, NT, preferred_element_type=F32)
            value = value.reshape(2, ROWS, 2 * CH)
            part[2 * j, pl.ds(2 * k, 2)] = value[:, :, :CH]
            part[2 * j + 1, pl.ds(2 * k, 2)] = value[:, :, CH:]
            return carry

        lax.fori_loop(0, NZ // 2, block, 0)

    def base_step(p, s):
        for h in range(2):
            ch = 2 * p + h
            if s == 0:
                base_first(ch, h, 0)
            else:
                base_forward(ch, h, s)
                if s == 1:
                    base_first(ch, 1 - h, s)
                else:
                    base_forward(ch, 1 - h, s)

    def adapter_part(s):
        for k in range(2):
            if s == 0:
                adapter_first(k, k, 0)
            else:
                adapter_forward(k, k, s)
                if s == 1:
                    adapter_first(k, 1 - k, s)
                else:
                    adapter_forward(k, 1 - k, s)

    def pair_of(i):
        return jnp.where(i > GITEM, i - 1, i)

    def is_pair(i):
        return (i >= 0) & (i < ITEMS) & (i != GITEM)

    def item_step(i, s):
        @pl.when(is_pair(i))
        def _():
            base_step(pair_of(i), s)

        @pl.when(i == GITEM)
        def _():
            adapter_part(s)

    def item(i, carry):
        @pl.when(is_pair(i) & (pair_of(i) + EARLY_W < NPAIR))
        def _():
            w_copy(pair_of(i) + EARLY_W).start()

        for s in (3, 2, 1):
            item_step(i - s, s)

        @pl.when(is_pair(i))
        def _():
            p = pair_of(i)

            product(p)

        @pl.when(i == GITEM)
        def _():
            adapter_grads()

        item_step(i, 0)

        @pl.when(is_pair(i - 4))
        def _():
            for h in range(2):
                base_last(2 * pair_of(i - 4) + h)

        @pl.when(i - 4 == GITEM)
        def _():
            for k in range(2):
                adapter_last(k)
            far_grads().start()

        return carry

    lax.fori_loop(0, ITEMS + 4, item, 0)

    far_grads().wait_recv()
    og_ref[pl.ds(yh, 1)] = tg[pl.ds(yh, 1)]
    og_ref[pl.ds(far_half, 1)] = gr[...].astype(F32)[None]

    def sent(block, sem):
        copy(block, block, sem, k_r, far_dev).wait_send()

    far_grads().wait_send()
    sums_copy().wait_send()
    half_copy().wait_send()
    sent(gf.at[0, 0 : NZ - 1], z_s)
    sent(lb.at[1:8], l_s)
    side_copy().wait_send()
    sent(gf.at[0 : NX - 1], x_s)
    sent(gf.at[0 : NZ // 2], c_s)
    sent(w2, w_s)
    for k in range(2):
        for d in range(2):
            for s in range(4):
                if s > 0 or d == k % 2:
                    a_copy(rg.at[d, k, s], d, k, s).wait_send()
    sent(part.at[0 : NCH // 2, 0 : NZ - 1], b_s)


def finish(hg_ref, og_ref, gate_ref, up_ref, ogate_ref, oup_ref, oga_ref, ogb_ref):
    for h in range(2):
        oga_ref[:, h * FH : (h + 1) * FH] = og_ref[h, :, :FH]
        ogb_ref[:, h * GH : (h + 1) * GH] = og_ref[h, :, FH:]

    def step(k, carry):
        cols = pl.ds(pl.multiple_of(k * 256, 256), 256)
        grad = hg_ref[:, cols]
        gate = gate_ref[:, cols].astype(F32)
        up_value = up_ref[:, cols].astype(F32)
        s = sigmoid(gate)
        oup_ref[:, cols] = (grad * gate * s).astype(BF16)
        ogate_ref[:, cols] = (grad * up_value * s * (1.0 + gate * (1.0 - s))).astype(BF16)
        return carry

    lax.fori_loop(0, HID // 256, step, 0)


def on_device(grad, weight, gate, up, down_factor, up_factor, owner, live):
    dma = pltpu.SemaphoreType.DMA
    vmem = pltpu.VMEM
    whole = pl.BlockSpec(memory_space=pltpu.VMEM)
    anywhere = pl.BlockSpec(memory_space=pl.ANY)
    hidden_grad, adapter_grads = pl.pallas_call(
        kernel,
        out_shape=(
            jax.ShapeDtypeStruct((ROWS, HID), F32),
            jax.ShapeDtypeStruct((2, RANK, GHALF), F32),
        ),
        in_specs=[anywhere] * 6 + [whole] * 2,
        out_specs=(whole,) * 2,
        scratch_shapes=[
            vmem((HID, KG), BF16),
            vmem((AR, HID), BF16),
            vmem((AR, KG), BF16),
            vmem((ROWS, HID), BF16),
            vmem((ROWS, HID), BF16),
            vmem((TILE, 16 * KG), BF16),
            vmem((NZ, TILE, 2 * KG), BF16),
            vmem((NZ, 8, TILE, 2 * KG), BF16),
            vmem((HID, KG), BF16),
            vmem((ROWS, HID), BF16),
            vmem((NCH, NZ, ROWS, CH), F32),
            vmem((2, NCH, 4, ROWS, CH), BF16),
            vmem((NCH, 2, ROWS, CH), BF16),
            vmem((ADAPTERS, RANK, GHALF), F32),
            vmem((2, 2, 4, RANK, GHALF), BF16),
            vmem((2, 2, RANK, GHALF), BF16),
            vmem((ROWS, GHALF), BF16),
            vmem((2, ROWS, GHALF), BF16),
            vmem((2, AR, 2 * ROWS), BF16),
            vmem((2, 2 * RANK, ROWS), BF16),
            vmem((2, RANK, GHALF), F32),
            vmem((2, RANK, GHALF), BF16),
            vmem((RANK, GHALF), BF16),
            vmem((ROWS, KG), BF16),
            vmem((ROWS, HID), F32),
            vmem((8, 2 * RANK, ROWS), F32),
            vmem((2, 2 * RANK, ROWS), F32),
            vmem((2, AR, ROWS), F32),
            dma((7,)),
            dma, dma((NPAIR,)),
            dma, dma((NZ,)),
            dma, dma((NX, NZ)),
            dma, dma((NZ,)),
            dma, dma((8,)),
            dma, dma,
            dma, dma((2, NCH, 4)),
            dma((2, 2, 4)), dma((2, 2, 4)),
            dma, dma,
            dma, dma,
            dma, dma,
        ],
        compiler_params=pltpu.CompilerParams(
            collective_id=0, has_side_effects=True, vmem_limit_bytes=60 * 1024 * 1024
        ),
    )(
        grad, weight, gate, up,
        down_factor.reshape(AR, HID), up_factor.reshape(AR, KG),
        owner.reshape(1, owner.shape[0]), live.reshape(1, live.shape[0]),
    )
    out_gate, out_up, grad_a, grad_b = pl.pallas_call(
        finish,
        out_shape=(
            jax.ShapeDtypeStruct((ROWS, HID), BF16),
            jax.ShapeDtypeStruct((ROWS, HID), BF16),
            jax.ShapeDtypeStruct((RANK, HID), F32),
            jax.ShapeDtypeStruct((RANK, KG), F32),
        ),
        in_specs=[whole] * 4,
        out_specs=(whole,) * 4,
    )(hidden_grad, adapter_grads, gate, up)
    return out_gate, out_up, grad_a[None], grad_b[None]


def solution(mesh):
    placed = (
        P("wa", None),
        P("dev", "wa"),
        P("wa", "dev"),
        P("wa", "dev"),
        P(None, None, "dev"),
        P(None, None, "dev"),
        P(),
        P(),
    )
    return jax.shard_map(
        on_device,
        mesh=mesh,
        in_specs=placed,
        out_specs=(P("wa", "dev"), P("wa", "dev"), P("wa", None, "dev"), P("wa", None, "dev")),
        check_vma=False,
    )
```

```python
import jax
import jax.numpy as jnp
from jax import lax
from jax.experimental import pallas as pl
from jax.experimental.pallas import tpu as pltpu
from jax.sharding import PartitionSpec as P

TILE = 16
NZ, NY, NX, NC = 8, 4, 4, 2
NDEV = 16
ROWS = 128
KG = 512
HID = 1792
CH = 128
NCH = HID // CH
NPAIR = NCH // 2
GCOL = HID + 512
GHALF = GCOL // 2
EARLY_W = 3
FH = HID // 2
GH = KG // 2
RANK = 16
ADAPTERS = 16
AR = RANK * ADAPTERS
MESH = pl.DeviceIdType.MESH
NT = (((1,), (1,)), ((), ()))
F32 = jnp.float32
BF16 = jnp.bfloat16
OFFSETS = (0, 1, 7, 2, 6, 3, 5, 4)


def sigmoid(v):
    return 1.0 / (1.0 + jnp.exp(-v))


def kernel(
    g_any, w_any, gate_any, up_any, a_any, b_any, owner_ref, live_ref,
    hg_ref, og_ref,
    w_ref, a_ref, b_ref, gate_ref, up_ref, gsh,
    gs, gf, w2, hid, part, rbuf, sbuf, pg, rg, sg, hs, hx, so, lx, tg, tb, gr, gsl, lo, lb, ls, sel,
    ld, w_s, w_r, z_s, z_r, x_s, x_r, c_s, c_r, l_s, l_r, t_s, t_r,
    b_s, b_r, a_s, a_r, h_s, h_r, k_s, k_r, y_s, y_r,
):
    wa = lax.axis_index("wa")
    dev = lax.axis_index("dev")
    yh, z = lax.div(wa, NZ), lax.rem(wa, NZ)
    yl, low = lax.div(dev, 8), lax.rem(dev, 8)
    x, c = lax.div(low, 2), lax.rem(low, 2)
    sh = c * 4 + x

    far_dev = ((1 - yh) * NZ + z, dev)

    def z_device(off):
        return (yh * NZ + lax.rem(z + off, NZ), dev)

    def x_index(step):
        return lax.rem(x + step, NX)

    def x_device(step):
        return (wa, yl * 8 + x_index(step) * 2 + c)

    core_dev = (wa, yl * 8 + x * 2 + (1 - c))

    def low_device(off):
        return (wa, yl * 8 + lax.rem(low + off, 8))

    side_dev = (wa, lax.rem(dev + 8, NDEV))

    def copy(src, dst, ssem, rsem, target):
        return pltpu.make_async_remote_copy(
            src_ref=src, dst_ref=dst, send_sem=ssem, recv_sem=rsem,
            device_id=target, device_id_type=MESH,
        )

    barrier = pltpu.get_barrier_semaphore()
    peers = [z_device(o) for o in (4, 3, 5, 2, 6, 1, 7)] + [far_dev, side_dev]
    peers += [low_device(o) for o in range(1, 8)]
    for peer in peers:
        pl.semaphore_signal(barrier, inc=1, device_id=peer, device_id_type=MESH)

    own_cols = pl.ds(pl.multiple_of(dev * KG, KG), KG)
    share_rows = pl.ds(pl.multiple_of(sh * TILE, TILE), TILE)
    loads = [
        pltpu.make_async_copy(src, dst, ld.at[i])
        for i, (src, dst) in enumerate(
            (
                (g_any.at[share_rows], gsh),
                (gate_any, gate_ref),
                (up_any, up_ref),
                (a_any, a_ref),
                (g_any.at[:, own_cols], gsl),
                (b_any, b_ref),
                (w_any, w_ref),
            )
        )
    ]
    for load in loads:
        load.start()

    live = live_ref[...].astype(F32)
    tile_lane = lax.broadcasted_iota(jnp.int32, (1, 128), 1)
    share_live = jnp.sum(
        jnp.where(tile_lane == wa * 8 + sh, live, 0.0), axis=1, keepdims=True
    )
    row16 = lax.broadcasted_iota(jnp.int32, (TILE, KG), 0).astype(F32)
    keep16 = row16 < share_live
    loads[0].wait()
    for q in range(NZ):
        for h in range(2):
            group = (yh if h == 0 else 1 - yh) * NZ + q
            cols = pl.ds(pl.multiple_of(group * KG, KG), KG)
            piece = jnp.where(keep16, gsh[:, cols], jnp.zeros((), BF16))
            gs[q, :, h * KG : (h + 1) * KG] = piece
    gf[pl.ds(z, 1), pl.ds(sh, 1)] = gs[pl.ds(z, 1)].reshape(1, 1, TILE, 2 * KG)

    def hidden_step(k, acc):
        cols = pl.ds(pl.multiple_of(k * 256, 256), 256)
        gate = gate_ref[:, cols].astype(F32)
        value = (gate * sigmoid(gate) * up_ref[:, cols].astype(F32)).astype(BF16)
        hid[:, cols] = value
        return acc + lax.dot_general(a_ref[:, cols], value, NT, preferred_element_type=F32)

    for i in (1, 2, 3):
        loads[i].wait()
    in_full = lax.fori_loop(0, HID // 256, hidden_step, jnp.zeros((AR, ROWS), F32))
    lane_tile = lax.broadcasted_iota(jnp.int32, (ROWS, 128), 1)
    sub_row = lax.broadcasted_iota(jnp.int32, (ROWS, 128), 0)
    pick = lane_tile == wa * 8 + lax.shift_right_logical(sub_row, 4)
    row_live = jnp.sum(jnp.where(pick, live, 0.0), axis=1, keepdims=True)
    position = lax.rem(lax.broadcasted_iota(jnp.int32, (ROWS, KG), 0), TILE).astype(F32)
    loads[4].wait()
    sliced = jnp.where(position < row_live, gsl[...], jnp.zeros((), BF16))
    gsl[...] = sliced
    loads[5].wait()
    out_full = lax.dot_general(b_ref[...], sliced, NT, preferred_element_type=F32)
    far_half = 1 - yh
    hs[:, :FH] = hid[:, pl.ds(pl.multiple_of(far_half * FH, 128), FH)]
    hs[:, FH:] = gsl[:, pl.ds(pl.multiple_of(far_half * GH, 128), GH)]
    hx[0, :, :FH] = hid[:, pl.ds(pl.multiple_of(yh * FH, 128), FH)]
    hx[0, :, FH:] = gsl[:, pl.ds(pl.multiple_of(yh * GH, 128), GH)]
    owners = jnp.broadcast_to(owner_ref[...].astype(F32), (8, 128)).astype(BF16)
    adapter_row = lax.shift_right_logical(
        lax.broadcasted_iota(jnp.int32, (AR, ROWS), 0), 4
    ).astype(F32)

    def select(group):
        pick_t = sub_row == group * 8 + lax.shift_right_logical(lane_tile, 4)
        chosen = jnp.where(pick_t, 1.0, 0.0).astype(BF16)
        owner_lane = jnp.dot(owners, chosen, preferred_element_type=F32)[0:1]
        return jnp.where(adapter_row == owner_lane, 1.0, 0.0)

    selected = select(wa)
    sel[0] = selected
    sel[1] = select(far_half * NZ + z)

    def choose(full):
        kept = jnp.where(selected > 0.5, full, 0.0)
        return jnp.sum(kept.reshape(ADAPTERS, RANK, ROWS), axis=0)

    lb[0, 0:RANK] = choose(in_full)
    lb[0, RANK : 2 * RANK] = choose(out_full)

    def l_copy(off):
        return copy(lb.at[0], lb.at[off], l_s, l_r.at[off], low_device(off))

    def w_copy(j):
        rows = pl.ds(pl.multiple_of(j * 2 * CH, 2 * CH), 2 * CH)
        return copy(w_any.at[rows], w2.at[rows], w_s, w_r.at[j], far_dev)

    def z_send(off):
        zt = lax.rem(z + off, NZ)
        return copy(gs.at[zt], gf.at[z, sh], z_s, z_r.at[off], z_device(off))

    def source(q):
        return lax.rem(z + OFFSETS[q], NZ)

    def x_send(q, step):
        band = gf.at[source(q), sh]
        return copy(band, band, x_s, x_r.at[step, q], x_device(step))

    def x_recv(q, step):
        band = gf.at[source(q), c * 4 + x_index(NX - step)]
        return copy(band, band, x_s, x_r.at[step, q], x_device(step))

    def core_send(q):
        block = gf.at[source(q), pl.ds(c * 4, 4)]
        return copy(block, block, c_s, c_r.at[q], core_dev)

    def core_recv(q):
        block = gf.at[source(q), pl.ds((1 - c) * 4, 4)]
        return copy(block, block, c_s, c_r.at[q], core_dev)

    pl.semaphore_wait(barrier, len(peers))
    for off in (1, 7, 2, 6, 3, 5, 4):
        z_send(off).start()
    for off in range(1, 8):
        l_copy(off).start()

    def half_copy():
        return copy(hs, hx.at[1], h_s, h_r, far_dev)

    half_copy().start()

    def side_copy():
        return copy(ls.at[0], ls.at[1], t_s, t_r, side_dev)

    for q in range(NZ):
        if q > 0:
            off = NZ - OFFSETS[q]
            band = gf.at[source(q), sh]
            copy(band, band, z_s, z_r.at[off], z_device(off)).wait_recv()
        for step in (1, 3, 2):
            x_send(q, step).start()
        if q == 2:
            for off in range(1, 8):
                l_copy(off).wait_recv()
            part_sum = jnp.zeros((2 * RANK, ROWS), F32)
            for src in range(8):
                part_sum = part_sum + lb[lax.rem(low + 8 - src, 8)]
            ls[0] = part_sum
            side_copy().start()

    side_copy().wait_recv()
    total = ls[0] + ls[1]
    lx[0] = total.astype(BF16)

    def sums_copy():
        return copy(lx.at[0], lx.at[1], k_s, k_r, far_dev)

    sums_copy().start()
    for j in range(EARLY_W):
        w_copy(j).start()

    def spread(which, first):
        values = lx[which, first : first + RANK].astype(F32)
        wide = jnp.broadcast_to(values[None], (ADAPTERS, RANK, ROWS)).reshape(AR, ROWS)
        return jnp.where(sel[which] > 0.5, wide, 0.0)

    spread_out_wide = spread(0, RANK)
    so[0, :, :ROWS] = spread(0, 0).astype(BF16)
    so[1, :, :ROWS] = spread_out_wide.astype(BF16)
    spread_out_t = spread_out_wide.T.astype(BF16)

    def adapter_step(k, carry):
        cols = pl.ds(pl.multiple_of(k * 256, 256), 256)
        lo[:, cols] = 2.0 * jnp.dot(spread_out_t, a_ref[:, cols], preferred_element_type=F32)
        return carry

    lax.fori_loop(0, HID // 256, adapter_step, 0)

    def adapter_grads():
        sums_copy().wait_recv()
        half_copy().wait_recv()
        so[0, :, ROWS:] = spread(1, 0).astype(BF16)
        so[1, :, ROWS:] = spread(1, RANK).astype(BF16)

        def columns(which, cols, width):
            left = jnp.concatenate([hx[0, :, cols], hx[1, :, cols]], axis=0)
            grad = 2.0 * jnp.dot(so[which], left, preferred_element_type=F32)
            pg[:, :, cols] = grad.reshape(ADAPTERS, RANK, width)

        def grad_step(k, carry):
            columns(1, pl.ds(pl.multiple_of(k * 128, 128), 128), 128)
            return carry

        lax.fori_loop(0, FH // 128, grad_step, 0)
        columns(0, slice(FH, FH + GH), GH)

    def z_next(d):
        return (yh * NZ + lax.rem(z + 1 + 6 * d, NZ), dev)

    def target_z(d, s):
        return lax.rem(z + NZ + (4 - s) * (1 - 2 * d), NZ)

    def b_copy(src, d, ch, s):
        return copy(src, rbuf.at[d, ch, s], b_s, b_r.at[d, ch, s], z_next(d))

    def a_copy(src, d, k, s):
        return copy(src, rg.at[d, k, s], a_s.at[d, k, s], a_r.at[d, k, s], z_next(d))

    def base_first(ch, d, s):
        sbuf[ch, s] = part[ch, target_z(d, s)].astype(BF16)
        b_copy(sbuf.at[ch, s], d, ch, s).start()

    def base_forward(ch, d, s):
        slot = rbuf.at[d, ch, s - 1]
        b_copy(slot, d, ch, s - 1).wait_recv()
        slot[...] = (slot[...].astype(F32) + part[ch, target_z(d, s)]).astype(BF16)
        b_copy(slot, d, ch, s).start()

    def base_last(ch):
        for d in range(2):
            b_copy(rbuf.at[d, ch, 3], d, ch, 3).wait_recv()
        cols = pl.ds(pl.multiple_of(ch * CH, CH), CH)
        base = part[ch, z] + rbuf[0, ch, 3].astype(F32) + rbuf[1, ch, 3].astype(F32)
        hg_ref[:, cols] = base + lo[:, cols]

    def own_grads(k, zt):
        return pg[k * NZ + zt]

    def far_grads():
        return copy(tb.at[far_half], gr, y_s, y_r, far_dev)

    def adapter_first(k, d, s):
        sg[k, s] = own_grads(k, target_z(d, s)).astype(BF16)
        a_copy(sg.at[k, s], d, k, s).start()

    def adapter_forward(k, d, s):
        slot = rg.at[d, k, s - 1]
        a_copy(slot, d, k, s - 1).wait_recv()
        slot[...] = (slot[...].astype(F32) + own_grads(k, target_z(d, s))).astype(BF16)
        a_copy(slot, d, k, s).start()

    def adapter_last(k):
        for d in range(2):
            a_copy(rg.at[d, k, 3], d, k, 3).wait_recv()
        done = own_grads(k, z) + rg[0, k, 3].astype(F32) + rg[1, k, 3].astype(F32)
        tg[k] = done
        tb[k] = done.astype(BF16)

    def product(j):
        rows = pl.ds(pl.multiple_of(j * 2 * CH, 2 * CH), 2 * CH)
        w_copy(j).wait_recv()
        mine = w_ref[rows, :]
        other = w2[rows, :]

        def block(k, carry):
            left = gf[pl.ds(2 * k, 2)].reshape(2 * ROWS, 2 * KG)
            value = lax.dot_general(left[:, :KG], mine, NT, preferred_element_type=F32)
            value = value + lax.dot_general(left[:, KG:], other, NT, preferred_element_type=F32)
            value = value.reshape(2, ROWS, 2 * CH)
            part[2 * j, pl.ds(2 * k, 2)] = value[:, :, :CH]
            part[2 * j + 1, pl.ds(2 * k, 2)] = value[:, :, CH:]
            return carry

        lax.fori_loop(0, NZ // 2, block, 0)

    def base_step(p, s):
        for h in range(2):
            ch = 2 * p + h
            if s == 0:
                base_first(ch, h, 0)
            else:
                base_forward(ch, h, s)
                if s == 1:
                    base_first(ch, 1 - h, s)
                else:
                    base_forward(ch, 1 - h, s)

    def adapter_part(s):
        for k in range(2):
            if s == 0:
                adapter_first(k, k, 0)
            else:
                adapter_forward(k, k, s)
                if s == 1:
                    adapter_first(k, 1 - k, s)
                else:
                    adapter_forward(k, 1 - k, s)

    for q in range(NZ):
        for step in (1, 3, 2):
            x_recv(q, step).wait_recv()
        core_send(q).start()
    adapter_grads()
    adapter_part(0)
    for q in range(NZ):
        core_recv(q).wait_recv()
    loads[6].wait()

    def item_step(p, s):
        @pl.when((p >= 0) & (p < NPAIR))
        def _():
            base_step(p, s)

    def item(i, carry):
        @pl.when(i + EARLY_W < NPAIR)
        def _():
            w_copy(i + EARLY_W).start()

        for s in (3, 2, 1):
            item_step(i - s, s)

        @pl.when(i < NPAIR)
        def _():
            product(i)

        item_step(i, 0)

        for s in (1, 2, 3):
            @pl.when(i == s - 1)
            def _(s=s):
                adapter_part(s)

        @pl.when(i == 3)
        def _():
            for k in range(2):
                adapter_last(k)
            far_grads().start()

        @pl.when(i >= 4)
        def _():
            for h in range(2):
                base_last(2 * (i - 4) + h)

        return carry

    lax.fori_loop(0, NPAIR + 4, item, 0)

    far_grads().wait_recv()
    og_ref[pl.ds(yh, 1)] = tg[pl.ds(yh, 1)]
    og_ref[pl.ds(far_half, 1)] = gr[...].astype(F32)[None]

    def sent(block, sem):
        copy(block, block, sem, k_r, far_dev).wait_send()

    far_grads().wait_send()
    sums_copy().wait_send()
    half_copy().wait_send()
    sent(gf.at[0, 0 : NZ - 1], z_s)
    sent(lb.at[1:8], l_s)
    side_copy().wait_send()
    sent(gf.at[0 : NX - 1], x_s)
    sent(gf.at[0 : NZ // 2], c_s)
    sent(w2, w_s)
    for k in range(2):
        for d in range(2):
            for s in range(4):
                if s > 0 or d == k % 2:
                    a_copy(rg.at[d, k, s], d, k, s).wait_send()
    sent(part.at[0 : NCH // 2, 0 : NZ - 1], b_s)


def finish(hg_ref, og_ref, gate_ref, up_ref, ogate_ref, oup_ref, oga_ref, ogb_ref):
    oga_ref[...] = og_ref[0, :, :FH]
    ogb_ref[...] = og_ref[0, :, FH:]

    def step(k, carry):
        cols = pl.ds(pl.multiple_of(k * CH, CH), CH)
        grad = hg_ref[:, cols]
        gate = gate_ref[:, cols].astype(F32)
        up_value = up_ref[:, cols].astype(F32)
        s = sigmoid(gate)
        oup_ref[:, cols] = (grad * gate * s).astype(BF16)
        ogate_ref[:, cols] = (grad * up_value * s * (1.0 + gate * (1.0 - s))).astype(BF16)
        return carry

    lax.fori_loop(0, FH // CH, step, 0)


def on_device(grad, weight, gate, up, down_factor, up_factor, owner, live):
    dma = pltpu.SemaphoreType.DMA
    vmem = pltpu.VMEM
    whole = pl.BlockSpec(memory_space=pltpu.VMEM)
    anywhere = pl.BlockSpec(memory_space=pl.ANY)
    hidden_grad, adapter_grads = pl.pallas_call(
        kernel,
        out_shape=(
            jax.ShapeDtypeStruct((ROWS, HID), F32),
            jax.ShapeDtypeStruct((2, RANK, GHALF), F32),
        ),
        in_specs=[anywhere] * 6 + [whole] * 2,
        out_specs=(whole,) * 2,
        scratch_shapes=[
            vmem((HID, KG), BF16),
            vmem((AR, HID), BF16),
            vmem((AR, KG), BF16),
            vmem((ROWS, HID), BF16),
            vmem((ROWS, HID), BF16),
            vmem((TILE, 16 * KG), BF16),
            vmem((NZ, TILE, 2 * KG), BF16),
            vmem((NZ, 8, TILE, 2 * KG), BF16),
            vmem((HID, KG), BF16),
            vmem((ROWS, HID), BF16),
            vmem((NCH, NZ, ROWS, CH), F32),
            vmem((2, NCH, 4, ROWS, CH), BF16),
            vmem((NCH, 2, ROWS, CH), BF16),
            vmem((ADAPTERS, RANK, GHALF), F32),
            vmem((2, 2, 4, RANK, GHALF), BF16),
            vmem((2, 2, RANK, GHALF), BF16),
            vmem((ROWS, GHALF), BF16),
            vmem((2, ROWS, GHALF), BF16),
            vmem((2, AR, 2 * ROWS), BF16),
            vmem((2, 2 * RANK, ROWS), BF16),
            vmem((2, RANK, GHALF), F32),
            vmem((2, RANK, GHALF), BF16),
            vmem((RANK, GHALF), BF16),
            vmem((ROWS, KG), BF16),
            vmem((ROWS, HID), F32),
            vmem((8, 2 * RANK, ROWS), F32),
            vmem((2, 2 * RANK, ROWS), F32),
            vmem((2, AR, ROWS), F32),
            dma((7,)),
            dma, dma((NPAIR,)),
            dma, dma((NZ,)),
            dma, dma((NX, NZ)),
            dma, dma((NZ,)),
            dma, dma((8,)),
            dma, dma,
            dma, dma((2, NCH, 4)),
            dma((2, 2, 4)), dma((2, 2, 4)),
            dma, dma,
            dma, dma,
            dma, dma,
        ],
        compiler_params=pltpu.CompilerParams(
            collective_id=0, has_side_effects=True, vmem_limit_bytes=60 * 1024 * 1024
        ),
    )(
        grad, weight, gate, up,
        down_factor.reshape(AR, HID), up_factor.reshape(AR, KG),
        owner.reshape(1, owner.shape[0]), live.reshape(1, live.shape[0]),
    )
    wide = pl.BlockSpec((ROWS, FH), lambda h: (0, h))
    out_gate, out_up, grad_a, grad_b = pl.pallas_call(
        finish,
        out_shape=(
            jax.ShapeDtypeStruct((ROWS, HID), BF16),
            jax.ShapeDtypeStruct((ROWS, HID), BF16),
            jax.ShapeDtypeStruct((RANK, HID), F32),
            jax.ShapeDtypeStruct((RANK, KG), F32),
        ),
        grid=(2,),
        in_specs=[wide, pl.BlockSpec((1, RANK, GHALF), lambda h: (h, 0, 0)), wide, wide],
        out_specs=(
            wide,
            wide,
            pl.BlockSpec((RANK, FH), lambda h: (0, h)),
            pl.BlockSpec((RANK, GH), lambda h: (0, h)),
        ),
    )(hidden_grad, adapter_grads, gate, up)
    return out_gate, out_up, grad_a[None], grad_b[None]


def solution(mesh):
    placed = (
        P("wa", None),
        P("dev", "wa"),
        P("wa", "dev"),
        P("wa", "dev"),
        P(None, None, "dev"),
        P(None, None, "dev"),
        P(),
        P(),
    )
    return jax.shard_map(
        on_device,
        mesh=mesh,
        in_specs=placed,
        out_specs=(P("wa", "dev"), P("wa", "dev"), P("wa", None, "dev"), P("wa", None, "dev")),
        check_vma=False,
    )
```

```python
import jax
import jax.numpy as jnp
from jax import lax
from jax.experimental import pallas as pl
from jax.experimental.pallas import tpu as pltpu
from jax.sharding import PartitionSpec as P

TILE = 16
NZ, NY, NX, NC = 8, 4, 4, 2
NDEV = 16
ROWS = 128
KG = 512
HID = 1792
CH = 128
NCH = HID // CH
NPAIR = NCH // 2
GCOL = HID + 512
GHALF = GCOL // 2
EARLY_W = 4
FH = HID // 2
GH = KG // 2
RANK = 16
ADAPTERS = 16
AR = RANK * ADAPTERS
MESH = pl.DeviceIdType.MESH
NT = (((1,), (1,)), ((), ()))
F32 = jnp.float32
BF16 = jnp.bfloat16
OFFSETS = (0, 1, 7, 2, 6, 3, 5, 4)


def sigmoid(v):
    return 1.0 / (1.0 + jnp.exp(-v))


def kernel(
    g_any, w_any, gate_any, up_any, a_any, b_any, owner_ref, live_ref,
    hg_ref, og_ref,
    w_ref, a_ref, b_ref, gate_ref, up_ref, gsh,
    gs, gf, w2, hid, part, rbuf, sbuf, pg, rg, sg, hs, hx, so, lx, tg, tb, gr, gsl, lo, lb, ls, sel,
    ld, w_s, w_r, z_s, z_r, x_s, x_r, c_s, c_r, l_s, l_r, t_s, t_r,
    b_s, b_r, a_s, a_r, h_s, h_r, k_s, k_r, y_s, y_r,
):
    wa = lax.axis_index("wa")
    dev = lax.axis_index("dev")
    yh, z = lax.div(wa, NZ), lax.rem(wa, NZ)
    yl, low = lax.div(dev, 8), lax.rem(dev, 8)
    x, c = lax.div(low, 2), lax.rem(low, 2)
    sh = c * 4 + x

    far_dev = ((1 - yh) * NZ + z, dev)

    def z_device(off):
        return (yh * NZ + lax.rem(z + off, NZ), dev)

    def x_index(step):
        return lax.rem(x + step, NX)

    def x_device(step):
        return (wa, yl * 8 + x_index(step) * 2 + c)

    core_dev = (wa, yl * 8 + x * 2 + (1 - c))

    def low_device(off):
        return (wa, yl * 8 + lax.rem(low + off, 8))

    side_dev = (wa, lax.rem(dev + 8, NDEV))

    def copy(src, dst, ssem, rsem, target):
        return pltpu.make_async_remote_copy(
            src_ref=src, dst_ref=dst, send_sem=ssem, recv_sem=rsem,
            device_id=target, device_id_type=MESH,
        )

    barrier = pltpu.get_barrier_semaphore()
    peers = [z_device(o) for o in (4, 3, 5, 2, 6, 1, 7)] + [far_dev, side_dev]
    peers += [low_device(o) for o in range(1, 8)]
    for peer in peers:
        pl.semaphore_signal(barrier, inc=1, device_id=peer, device_id_type=MESH)

    own_cols = pl.ds(pl.multiple_of(dev * KG, KG), KG)
    share_rows = pl.ds(pl.multiple_of(sh * TILE, TILE), TILE)
    loads = [
        pltpu.make_async_copy(src, dst, ld.at[i])
        for i, (src, dst) in enumerate(
            (
                (g_any.at[share_rows], gsh),
                (gate_any, gate_ref),
                (up_any, up_ref),
                (a_any, a_ref),
                (g_any.at[:, own_cols], gsl),
                (b_any, b_ref),
                (w_any, w_ref),
            )
        )
    ]
    for load in loads:
        load.start()

    live = live_ref[...].astype(F32)
    tile_lane = lax.broadcasted_iota(jnp.int32, (1, 128), 1)
    share_live = jnp.sum(
        jnp.where(tile_lane == wa * 8 + sh, live, 0.0), axis=1, keepdims=True
    )
    row16 = lax.broadcasted_iota(jnp.int32, (TILE, KG), 0).astype(F32)
    keep16 = row16 < share_live
    loads[0].wait()
    for q in range(NZ):
        for h in range(2):
            group = (yh if h == 0 else 1 - yh) * NZ + q
            cols = pl.ds(pl.multiple_of(group * KG, KG), KG)
            piece = jnp.where(keep16, gsh[:, cols], jnp.zeros((), BF16))
            gs[q, :, h * KG : (h + 1) * KG] = piece
    gf[pl.ds(z, 1), pl.ds(sh, 1)] = gs[pl.ds(z, 1)].reshape(1, 1, TILE, 2 * KG)

    def hidden_step(k, acc):
        cols = pl.ds(pl.multiple_of(k * 256, 256), 256)
        gate = gate_ref[:, cols].astype(F32)
        value = (gate * sigmoid(gate) * up_ref[:, cols].astype(F32)).astype(BF16)
        hid[:, cols] = value
        return acc + lax.dot_general(a_ref[:, cols], value, NT, preferred_element_type=F32)

    for i in (1, 2, 3):
        loads[i].wait()
    in_full = lax.fori_loop(0, HID // 256, hidden_step, jnp.zeros((AR, ROWS), F32))
    lane_tile = lax.broadcasted_iota(jnp.int32, (ROWS, 128), 1)
    sub_row = lax.broadcasted_iota(jnp.int32, (ROWS, 128), 0)
    pick = lane_tile == wa * 8 + lax.shift_right_logical(sub_row, 4)
    row_live = jnp.sum(jnp.where(pick, live, 0.0), axis=1, keepdims=True)
    position = lax.rem(lax.broadcasted_iota(jnp.int32, (ROWS, KG), 0), TILE).astype(F32)
    loads[4].wait()
    sliced = jnp.where(position < row_live, gsl[...], jnp.zeros((), BF16))
    gsl[...] = sliced
    loads[5].wait()
    out_full = lax.dot_general(b_ref[...], sliced, NT, preferred_element_type=F32)
    far_half = 1 - yh
    hs[:, :FH] = hid[:, pl.ds(pl.multiple_of(far_half * FH, 128), FH)]
    hs[:, FH:] = gsl[:, pl.ds(pl.multiple_of(far_half * GH, 128), GH)]
    hx[0, :, :FH] = hid[:, pl.ds(pl.multiple_of(yh * FH, 128), FH)]
    hx[0, :, FH:] = gsl[:, pl.ds(pl.multiple_of(yh * GH, 128), GH)]
    owners = jnp.broadcast_to(owner_ref[...].astype(F32), (8, 128)).astype(BF16)
    adapter_row = lax.shift_right_logical(
        lax.broadcasted_iota(jnp.int32, (AR, ROWS), 0), 4
    ).astype(F32)

    def select(group):
        pick_t = sub_row == group * 8 + lax.shift_right_logical(lane_tile, 4)
        chosen = jnp.where(pick_t, 1.0, 0.0).astype(BF16)
        owner_lane = jnp.dot(owners, chosen, preferred_element_type=F32)[0:1]
        return jnp.where(adapter_row == owner_lane, 1.0, 0.0)

    selected = select(wa)
    sel[0] = selected
    sel[1] = select(far_half * NZ + z)

    def choose(full):
        kept = jnp.where(selected > 0.5, full, 0.0)
        return jnp.sum(kept.reshape(ADAPTERS, RANK, ROWS), axis=0)

    lb[0, 0:RANK] = choose(in_full)
    lb[0, RANK : 2 * RANK] = choose(out_full)

    def l_copy(off):
        return copy(lb.at[0], lb.at[off], l_s, l_r.at[off], low_device(off))

    def w_copy(j):
        rows = pl.ds(pl.multiple_of(j * 2 * CH, 2 * CH), 2 * CH)
        return copy(w_any.at[rows], w2.at[rows], w_s, w_r.at[j], far_dev)

    def z_send(off):
        zt = lax.rem(z + off, NZ)
        return copy(gs.at[zt], gf.at[z, sh], z_s, z_r.at[off], z_device(off))

    def source(q):
        return lax.rem(z + OFFSETS[q], NZ)

    def x_send(q, step):
        band = gf.at[source(q), sh]
        return copy(band, band, x_s, x_r.at[step, q], x_device(step))

    def x_recv(q, step):
        band = gf.at[source(q), c * 4 + x_index(NX - step)]
        return copy(band, band, x_s, x_r.at[step, q], x_device(step))

    def core_send(q):
        block = gf.at[source(q), pl.ds(c * 4, 4)]
        return copy(block, block, c_s, c_r.at[q], core_dev)

    def core_recv(q):
        block = gf.at[source(q), pl.ds((1 - c) * 4, 4)]
        return copy(block, block, c_s, c_r.at[q], core_dev)

    pl.semaphore_wait(barrier, len(peers))
    for off in (1, 7, 2, 6, 3, 5, 4):
        z_send(off).start()
    for off in range(1, 8):
        l_copy(off).start()

    def half_copy():
        return copy(hs, hx.at[1], h_s, h_r, far_dev)

    half_copy().start()

    def side_copy():
        return copy(ls.at[0], ls.at[1], t_s, t_r, side_dev)

    for q in range(NZ):
        if q > 0:
            off = NZ - OFFSETS[q]
            band = gf.at[source(q), sh]
            copy(band, band, z_s, z_r.at[off], z_device(off)).wait_recv()
        for step in (2, 1, 3):
            x_send(q, step).start()
        if q == 2:
            for off in range(1, 8):
                l_copy(off).wait_recv()
            part_sum = jnp.zeros((2 * RANK, ROWS), F32)
            for src in range(8):
                part_sum = part_sum + lb[lax.rem(low + 8 - src, 8)]
            ls[0] = part_sum
            side_copy().start()

    side_copy().wait_recv()
    total = ls[0] + ls[1]
    lx[0] = total.astype(BF16)

    def sums_copy():
        return copy(lx.at[0], lx.at[1], k_s, k_r, far_dev)

    sums_copy().start()
    for j in range(EARLY_W):
        w_copy(j).start()

    def spread(which, first):
        values = lx[which, first : first + RANK].astype(F32)
        wide = jnp.broadcast_to(values[None], (ADAPTERS, RANK, ROWS)).reshape(AR, ROWS)
        return jnp.where(sel[which] > 0.5, wide, 0.0)

    spread_out_wide = spread(0, RANK)
    so[0, :, :ROWS] = spread(0, 0).astype(BF16)
    so[1, :, :ROWS] = spread_out_wide.astype(BF16)
    spread_out_t = spread_out_wide.T.astype(BF16)

    def adapter_step(k, carry):
        cols = pl.ds(pl.multiple_of(k * 256, 256), 256)
        lo[:, cols] = 2.0 * jnp.dot(spread_out_t, a_ref[:, cols], preferred_element_type=F32)
        return carry

    lax.fori_loop(0, HID // 256, adapter_step, 0)

    def adapter_grads():
        sums_copy().wait_recv()
        half_copy().wait_recv()
        so[0, :, ROWS:] = spread(1, 0).astype(BF16)
        so[1, :, ROWS:] = spread(1, RANK).astype(BF16)

        def columns(which, cols, width):
            left = jnp.concatenate([hx[0, :, cols], hx[1, :, cols]], axis=0)
            grad = 2.0 * jnp.dot(so[which], left, preferred_element_type=F32)
            pg[:, :, cols] = grad.reshape(ADAPTERS, RANK, width)

        def grad_step(k, carry):
            columns(1, pl.ds(pl.multiple_of(k * 128, 128), 128), 128)
            return carry

        lax.fori_loop(0, FH // 128, grad_step, 0)
        columns(0, slice(FH, FH + GH), GH)

    def z_next(d):
        return (yh * NZ + lax.rem(z + 1 + 6 * d, NZ), dev)

    def target_z(d, s):
        return lax.rem(z + NZ + (4 - s) * (1 - 2 * d), NZ)

    def b_copy(src, d, ch, s):
        return copy(src, rbuf.at[d, ch, s], b_s, b_r.at[d, ch, s], z_next(d))

    def a_copy(src, d, k, s):
        return copy(src, rg.at[d, k, s], a_s.at[d, k, s], a_r.at[d, k, s], z_next(d))

    def base_first(ch, d, s):
        sbuf[ch, s] = part[ch, target_z(d, s)].astype(BF16)
        b_copy(sbuf.at[ch, s], d, ch, s).start()

    def base_forward(ch, d, s):
        slot = rbuf.at[d, ch, s - 1]
        b_copy(slot, d, ch, s - 1).wait_recv()
        slot[...] = (slot[...].astype(F32) + part[ch, target_z(d, s)]).astype(BF16)
        b_copy(slot, d, ch, s).start()

    def base_last(ch):
        for d in range(2):
            b_copy(rbuf.at[d, ch, 3], d, ch, 3).wait_recv()
        cols = pl.ds(pl.multiple_of(ch * CH, CH), CH)
        base = part[ch, z] + rbuf[0, ch, 3].astype(F32) + rbuf[1, ch, 3].astype(F32)
        hg_ref[:, cols] = base + lo[:, cols]

    def own_grads(k, zt):
        return pg[k * NZ + zt]

    def far_grads():
        return copy(tb.at[far_half], gr, y_s, y_r, far_dev)

    def adapter_first(k, d, s):
        sg[k, s] = own_grads(k, target_z(d, s)).astype(BF16)
        a_copy(sg.at[k, s], d, k, s).start()

    def adapter_forward(k, d, s):
        slot = rg.at[d, k, s - 1]
        a_copy(slot, d, k, s - 1).wait_recv()
        slot[...] = (slot[...].astype(F32) + own_grads(k, target_z(d, s))).astype(BF16)
        a_copy(slot, d, k, s).start()

    def adapter_last(k):
        for d in range(2):
            a_copy(rg.at[d, k, 3], d, k, 3).wait_recv()
        done = own_grads(k, z) + rg[0, k, 3].astype(F32) + rg[1, k, 3].astype(F32)
        tg[k] = done
        tb[k] = done.astype(BF16)

    def product(j):
        rows = pl.ds(pl.multiple_of(j * 2 * CH, 2 * CH), 2 * CH)
        w_copy(j).wait_recv()
        mine = w_ref[rows, :]
        other = w2[rows, :]

        def block(k, carry):
            left = gf[pl.ds(2 * k, 2)].reshape(2 * ROWS, 2 * KG)
            value = lax.dot_general(left[:, :KG], mine, NT, preferred_element_type=F32)
            value = value + lax.dot_general(left[:, KG:], other, NT, preferred_element_type=F32)
            value = value.reshape(2, ROWS, 2 * CH)
            part[2 * j, pl.ds(2 * k, 2)] = value[:, :, :CH]
            part[2 * j + 1, pl.ds(2 * k, 2)] = value[:, :, CH:]
            return carry

        lax.fori_loop(0, NZ // 2, block, 0)

    def base_step(p, s):
        for h in range(2):
            ch = 2 * p + h
            if s == 0:
                base_first(ch, h, 0)
            else:
                base_forward(ch, h, s)
                if s == 1:
                    base_first(ch, 1 - h, s)
                else:
                    base_forward(ch, 1 - h, s)

    def adapter_part(s):
        for k in range(2):
            if s == 0:
                adapter_first(k, k, 0)
            else:
                adapter_forward(k, k, s)
                if s == 1:
                    adapter_first(k, 1 - k, s)
                else:
                    adapter_forward(k, 1 - k, s)

    for q in range(NZ):
        for step in (2, 1, 3):
            x_recv(q, step).wait_recv()
        core_send(q).start()
    adapter_grads()
    adapter_part(0)
    for q in range(NZ):
        core_recv(q).wait_recv()
    loads[6].wait()

    def item_step(p, s):
        @pl.when((p >= 0) & (p < NPAIR))
        def _():
            base_step(p, s)

    def item(i, carry):
        @pl.when(i + EARLY_W < NPAIR)
        def _():
            w_copy(i + EARLY_W).start()

        for s in (3, 2, 1):
            item_step(i - s, s)

        @pl.when(i < NPAIR)
        def _():
            product(i)

        item_step(i, 0)

        for s in (1, 2, 3):
            @pl.when(i == s - 1)
            def _(s=s):
                adapter_part(s)

        @pl.when(i == 3)
        def _():
            for k in range(2):
                adapter_last(k)
            far_grads().start()

        @pl.when(i >= 4)
        def _():
            for h in range(2):
                base_last(2 * (i - 4) + h)

        return carry

    lax.fori_loop(0, NPAIR + 4, item, 0)

    far_grads().wait_recv()
    og_ref[pl.ds(yh, 1)] = tg[pl.ds(yh, 1)]
    og_ref[pl.ds(far_half, 1)] = gr[...].astype(F32)[None]

    def sent(block, sem):
        copy(block, block, sem, k_r, far_dev).wait_send()

    far_grads().wait_send()
    sums_copy().wait_send()
    half_copy().wait_send()
    sent(gf.at[0, 0 : NZ - 1], z_s)
    sent(lb.at[1:8], l_s)
    side_copy().wait_send()
    sent(gf.at[0 : NX - 1], x_s)
    sent(gf.at[0 : NZ // 2], c_s)
    sent(w2, w_s)
    for k in range(2):
        for d in range(2):
            for s in range(4):
                if s > 0 or d == k % 2:
                    a_copy(rg.at[d, k, s], d, k, s).wait_send()
    sent(part.at[0 : NCH // 2, 0 : NZ - 1], b_s)


def finish(hg_ref, og_ref, gate_ref, up_ref, ogate_ref, oup_ref, oga_ref, ogb_ref):
    oga_ref[...] = og_ref[0, :, :FH]
    ogb_ref[...] = og_ref[0, :, FH:]

    def step(k, carry):
        cols = pl.ds(pl.multiple_of(k * CH, CH), CH)
        grad = hg_ref[:, cols]
        gate = gate_ref[:, cols].astype(F32)
        up_value = up_ref[:, cols].astype(F32)
        s = sigmoid(gate)
        oup_ref[:, cols] = (grad * gate * s).astype(BF16)
        ogate_ref[:, cols] = (grad * up_value * s * (1.0 + gate * (1.0 - s))).astype(BF16)
        return carry

    lax.fori_loop(0, FH // CH, step, 0)


def on_device(grad, weight, gate, up, down_factor, up_factor, owner, live):
    dma = pltpu.SemaphoreType.DMA
    vmem = pltpu.VMEM
    whole = pl.BlockSpec(memory_space=pltpu.VMEM)
    anywhere = pl.BlockSpec(memory_space=pl.ANY)
    hidden_grad, adapter_grads = pl.pallas_call(
        kernel,
        out_shape=(
            jax.ShapeDtypeStruct((ROWS, HID), F32),
            jax.ShapeDtypeStruct((2, RANK, GHALF), F32),
        ),
        in_specs=[anywhere] * 6 + [whole] * 2,
        out_specs=(whole,) * 2,
        scratch_shapes=[
            vmem((HID, KG), BF16),
            vmem((AR, HID), BF16),
            vmem((AR, KG), BF16),
            vmem((ROWS, HID), BF16),
            vmem((ROWS, HID), BF16),
            vmem((TILE, 16 * KG), BF16),
            vmem((NZ, TILE, 2 * KG), BF16),
            vmem((NZ, 8, TILE, 2 * KG), BF16),
            vmem((HID, KG), BF16),
            vmem((ROWS, HID), BF16),
            vmem((NCH, NZ, ROWS, CH), F32),
            vmem((2, NCH, 4, ROWS, CH), BF16),
            vmem((NCH, 2, ROWS, CH), BF16),
            vmem((ADAPTERS, RANK, GHALF), F32),
            vmem((2, 2, 4, RANK, GHALF), BF16),
            vmem((2, 2, RANK, GHALF), BF16),
            vmem((ROWS, GHALF), BF16),
            vmem((2, ROWS, GHALF), BF16),
            vmem((2, AR, 2 * ROWS), BF16),
            vmem((2, 2 * RANK, ROWS), BF16),
            vmem((2, RANK, GHALF), F32),
            vmem((2, RANK, GHALF), BF16),
            vmem((RANK, GHALF), BF16),
            vmem((ROWS, KG), BF16),
            vmem((ROWS, HID), F32),
            vmem((8, 2 * RANK, ROWS), F32),
            vmem((2, 2 * RANK, ROWS), F32),
            vmem((2, AR, ROWS), F32),
            dma((7,)),
            dma, dma((NPAIR,)),
            dma, dma((NZ,)),
            dma, dma((NX, NZ)),
            dma, dma((NZ,)),
            dma, dma((8,)),
            dma, dma,
            dma, dma((2, NCH, 4)),
            dma((2, 2, 4)), dma((2, 2, 4)),
            dma, dma,
            dma, dma,
            dma, dma,
        ],
        compiler_params=pltpu.CompilerParams(
            collective_id=0, has_side_effects=True, vmem_limit_bytes=60 * 1024 * 1024
        ),
    )(
        grad, weight, gate, up,
        down_factor.reshape(AR, HID), up_factor.reshape(AR, KG),
        owner.reshape(1, owner.shape[0]), live.reshape(1, live.shape[0]),
    )
    wide = pl.BlockSpec((ROWS, FH), lambda h: (0, h))
    out_gate, out_up, grad_a, grad_b = pl.pallas_call(
        finish,
        out_shape=(
            jax.ShapeDtypeStruct((ROWS, HID), BF16),
            jax.ShapeDtypeStruct((ROWS, HID), BF16),
            jax.ShapeDtypeStruct((RANK, HID), F32),
            jax.ShapeDtypeStruct((RANK, KG), F32),
        ),
        grid=(2,),
        in_specs=[wide, pl.BlockSpec((1, RANK, GHALF), lambda h: (h, 0, 0)), wide, wide],
        out_specs=(
            wide,
            wide,
            pl.BlockSpec((RANK, FH), lambda h: (0, h)),
            pl.BlockSpec((RANK, GH), lambda h: (0, h)),
        ),
    )(hidden_grad, adapter_grads, gate, up)
    return out_gate, out_up, grad_a[None], grad_b[None]


def solution(mesh):
    placed = (
        P("wa", None),
        P("dev", "wa"),
        P("wa", "dev"),
        P("wa", "dev"),
        P(None, None, "dev"),
        P(None, None, "dev"),
        P(),
        P(),
    )
    return jax.shard_map(
        on_device,
        mesh=mesh,
        in_specs=placed,
        out_specs=(P("wa", "dev"), P("wa", "dev"), P("wa", None, "dev"), P("wa", None, "dev")),
        check_vma=False,
    )
```
